256 devices in a mesh: slab: 64 (over y, x_lo, z), grp: 4 (over x_hi, core).
Axes of the slice: x: 4 (x_hi: 2, x_lo: 2; x = x_hi * 2 + x_lo), y: 4, z: 8, core: 2. Of those that a mesh axis runs over, the one named last changes fastest.
Arguments:
- tiles: bfloat16 [768, 27, 36864], P(('slab', 'grp')), may hold values from -0.0390625 to 0.0390625
- neighbours: int32 [768, 27], P('slab'), may hold values from 0 to 767, as said below
- t_cur: bfloat16 [768, 192, 512], P('slab', None, 'grp'), may hold values from -6 to 6
- t_prev: float32 [768, 192, 512], P('slab', None, 'grp'), may hold values from -6 to 6
- probes: float32 [768, 192, 512], P('slab', None, 'grp'), may hold values from -18 to 18
Outputs:
- t_next: float32 [768, 192, 512], P('slab', None, 'grp')
- moments: float32 [2, 512], P(None, 'grp')
The draws below stay inside these ranges and needn't reach their ends.
Inputs may be any that keep to these rules, and one draw needn't show every extreme that they name: Block b lies in slab b // 12; each of its neighbours lies in the same slab or in one of the two slabs beside it, the last slab being beside the first.
All inputs are finite; a program needn't handle non-finite values.
Results may differ from the reference program's by a relative error of at most 0.0003.
Values may be sent and summed in bfloat16 or wider, within the bound.
A program may use at most 192 MiB of HBM per device.

```python
import math
import jax
import jax.numpy as jnp
from jax import lax

BS = 192
NEIGH = 27
BY = 3
BZ = 4
PROBES = 512
BPS = 12
NBLK = 768


def draw_neighbours(key, part):
    slabs = NBLK // BPS
    keys = jax.random.split(jax.random.fold_in(key, 11), slabs)
    perms = jax.vmap(lambda k: jax.random.permutation(k, BPS))(keys).astype(jnp.int32)
    inverse = jnp.argsort(perms, axis=1).astype(jnp.int32)
    block = jnp.arange(NBLK, dtype=jnp.int32)
    slab_of = block // BPS
    place = perms[slab_of, block % BPS]
    ycoord = place // BZ
    zcoord = place % BZ
    offs = jnp.arange(27, dtype=jnp.int32)
    shift_x = offs // 9 - 1
    shift_y = offs // 3 % 3 - 1
    shift_z = offs % 3 - 1
    near_slab = (slab_of[:, None] + shift_x[None, :]) % slabs
    near_place = (ycoord[:, None] + shift_y[None, :]) % BY * BZ + (zcoord[:, None] + shift_z[None, :]) % BZ
    near = near_slab * BPS + inverse[near_slab, near_place]
    okeys = jax.random.split(jax.random.fold_in(key, 12), NBLK)
    orders = jax.vmap(lambda k: jax.random.permutation(k, 27))(okeys).astype(jnp.int32)
    return jnp.take_along_axis(near, orders, axis=1).astype(jnp.int32)


def draw_probes(key, part):
    slabs = NBLK // BPS
    block = jnp.arange(NBLK, dtype=jnp.int32)
    ramp = 1.0 + 2.0 * (block // BPS).astype(jnp.float32) / (slabs - 1)
    ramp = ramp[:, None, None]
    base = jax.random.normal(jax.random.fold_in(key, 22), (NBLK, BS, PROBES), jnp.float32)
    values = jnp.clip(base, -6.0, 6.0) * ramp
    return values.astype(jnp.float32)


def block_levels(key, extent, pieces, smallest, top_value):
    level, own = 1.0, jax.random.fold_in(key, 6)
    for position, blocks in pieces:
        steps = jnp.exp(jax.random.uniform(jax.random.fold_in(own, position), (blocks,), jnp.float32, smallest / len(pieces), top_value / len(pieces)))
        level = level * jnp.repeat(steps, extent[position] // blocks).reshape([-1 if axis == position else 1 for axis in range(len(extent))])
    return level


def normal_values(key, dims, spread, limit, cuts=(), held_as=jnp.bfloat16):
    values = spread * jax.random.normal(key, dims, jnp.float32)
    if cuts:
        values = values * block_levels(key, dims, cuts, -0.22, 0.18)
    return jnp.clip(values, -limit, limit).astype(held_as)


def setup_inputs(seed: int = 0) -> dict:
    streams_of = jax.random.split(jax.random.key(seed), 6)
    return {
        "tiles": normal_values(streams_of[0], (NBLK, NEIGH, BS * BS), (4 * NEIGH * BS) ** -0.5, 0.0390625, ((0, 256),)),
        "neighbours": draw_neighbours(jax.random.fold_in(streams_of[5], 71), 0),
        "t_cur": normal_values(streams_of[2], (NBLK, BS, PROBES), 1.0, 6.0, ((0, 64), (2, 4))),
        "t_prev": normal_values(streams_of[3], (NBLK, BS, PROBES), 1.0, 6.0, ((0, 64), (2, 4)), jnp.float32),
        "probes": draw_probes(jax.random.fold_in(streams_of[5], 71), 0),
    }


def reference(tiles, neighbours, t_cur, t_prev, probes):
    current = t_cur.astype(jnp.float32)

    def one_block(pair):
        tile_row, nbr = pair
        square = tile_row.astype(jnp.float32).reshape((NEIGH, BS, BS))
        near = current[nbr.astype(jnp.int32)]
        return jnp.einsum('krc,kcp->rp', square, near)
    image = lax.map(one_block, (tiles, neighbours))
    t_next = 2.0 * image - t_prev
    factor = 1.0 / math.sqrt(NBLK * BS)
    first = lax.optimization_barrier(jnp.sum(probes * t_next, axis=(0, 1))) * factor
    second = lax.optimization_barrier(jnp.sum(current * t_next, axis=(0, 1))) * factor
    return (t_next, jnp.stack([first, second]))
```

```python
import functools
import math

import jax
import jax.numpy as jnp
from jax import lax
from jax.experimental import pallas as pl
from jax.experimental.pallas import tpu as pltpu
from jax.sharding import PartitionSpec as P

MESH = pl.DeviceIdType.MESH
BPS, BS, NB = 12, 192, 27
MINE = 3
COLS = 128
LANES = 128
FLAT = BS * BS // LANES
PITCH = FLAT + 1
KPAD = 5248
CHUNKS = 4
CB = BPS // CHUNKS
SLABS, ZS = 64, 8


class Sems:
    def __init__(self):
        self.n = 0

    def take(self, *dims):
        size = math.prod(dims) if dims else 1
        start = self.n
        self.n += size
        return start


RX = Sems()
EX, OWN, EXC = RX.take(CHUNKS), RX.take(), RX.take(CHUNKS)
NEAR, FAR, NEARC, FARC = [RX.take(2, CHUNKS) for _ in range(4)]
IMG, M1, M2 = RX.take(3), RX.take(8), RX.take(8)
NSEM = RX.n


def relayout(x, stage, a, b, part, parts):
    per = FLAT // parts
    step = 12

    def spread(m, carry):
        for u in range(step):
            j = part * per + m * step + u
            v = x[b, :, pl.ds(pl.multiple_of(j * LANES, LANES), LANES)]
            stage[pl.ds(j, NB, stride=PITCH), :] = v.astype(jnp.float32)
        return carry

    lax.fori_loop(0, per // step, spread, 0)


def assemble(stage, a, b):
    low = lax.broadcasted_iota(jnp.int32, (BS // 2, LANES), 1) < 64
    load = lambda k, i: stage[pl.ds(k * PITCH + i, BS // 2, stride=3), :]
    turn = lambda v: pltpu.roll(v, 64, 1)

    def pair(p, last):
        k = 2 * p
        e0, e1, e2 = [load(k, i) for i in range(3)]
        if last:
            zero = jnp.zeros_like(e0)
            f1, f2, rf0, rf1 = zero, zero, zero, zero
        else:
            f0, f1, f2 = [load(k + 1, i) for i in range(3)]
            rf0, rf1 = turn(f0), turn(f1)
        re1, re2 = turn(e1), turn(e2)
        even = [e0, jnp.where(low, e1, rf0), jnp.where(low, rf0, rf1)]
        odd = [jnp.where(low, re1, re2), jnp.where(low, re2, f1), f2]
        for t in range(2 if last else 3):
            at = pl.ds(pl.multiple_of(p * 384 + 128 * t, 128), LANES)
            a[b, 0 : BS // 2, at] = even[t].astype(jnp.bfloat16)
            a[b, BS // 2 : BS, at] = odd[t].astype(jnp.bfloat16)

    def body(p, carry):
        pair(p, False)
        return carry

    lax.fori_loop(0, NB // 2, body, 0)
    pair(NB // 2, True)


def multiply(ids, a, near, out):
    def one(b, carry):
        def rhs(k):
            n = ids[b * NB + k]
            return jnp.concatenate([near[0, n], near[1, n]], axis=1)

        total = None
        for first in range(0, NB, 4):
            ks = range(first, min(first + 4, NB))
            parts = [rhs(k) for k in ks]
            if len(parts) == 3:
                parts.append(jnp.zeros((64, 2 * COLS), jnp.bfloat16))
            right = jnp.concatenate(parts, axis=0)
            left = a[b, :, first * BS : first * BS + right.shape[0]]
            term = jnp.dot(left, right, preferred_element_type=jnp.float32)
            total = term if total is None else total + term
        half = BS // 2
        for e in range(2):
            for c in range(2):
                out[c, b, pl.ds(e, half, stride=2), :] = total[
                    half * e : half * (e + 1), COLS * c : COLS * (c + 1)
                ]
        return carry

    lax.fori_loop(0, MINE, one, 0)


def kernel(
    neighbours, tiles, t_cur, t_prev, probes, t_next, moments,
    x, stage, a, near, far, out_far, out_near, image, prev, probe, ids, sums1, sums2,
    local, ssem, rsem,
):
    s, g = lax.axis_index("slab"), lax.axis_index("grp")
    z = lax.rem(s, ZS)
    row = lax.div(s, ZS)
    h, c = lax.div(g, 2), lax.rem(g, 2)
    up, down = lax.rem(s + 1, SLABS), lax.rem(s + SLABS - 1, SLABS)
    here = lambda hh, cc: (s, hh * 2 + cc)
    partner, across, cross = here(h, 1 - c), here(1 - h, c), here(1 - h, 1 - c)
    zpeer = lambda o: (row * ZS + lax.rem(z + o, ZS), g)
    rpeer = lambda o: (lax.rem(row + o, 8) * ZS + z, g)
    sides = (up, down)
    edge = (z == ZS - 1, z == 0)
    other = (1 - h) * 2 + c

    loads = [
        pltpu.make_async_copy(t_cur, near.at[c, pl.ds(BPS, BPS)], local.at[0]),
        pltpu.make_async_copy(t_prev, prev, local.at[1]),
        pltpu.make_async_copy(probes, probe, local.at[2]),
    ] + [pltpu.make_async_copy(tiles.at[b], x.at[b], local.at[3 + b]) for b in range(MINE)]

    barrier = pltpu.get_barrier_semaphore()
    peers = [partner, across, cross]
    peers += [(side, g) for side in sides] + [(side, other) for side in sides]
    peers += [zpeer(o) for o in range(1, ZS)] + [rpeer(o) for o in range(1, 8)]
    for peer in peers:
        pl.semaphore_signal(barrier, 1, device_id=peer, device_id_type=MESH)
    for load in loads:
        load.start()

    def indices(b, carry):
        for k in range(NB):
            n = neighbours[g * MINE + b, k]
            rel = lax.rem(lax.div(n, BPS) - s + 1 + SLABS, SLABS)
            ids[b * NB + k] = jnp.minimum(rel, 2) * BPS + lax.rem(n, BPS)
        return carry

    lax.fori_loop(0, MINE, indices, 0)
    pl.semaphore_wait(barrier, len(peers))

    def send(src, dst, sem, device):
        return pltpu.make_async_remote_copy(
            src, dst, ssem.at[sem], rsem.at[sem], device_id=device, device_id_type=MESH
        )

    def mine(i):
        return t_cur.at[pl.ds(i * CB, CB)]

    def slot(buf, col, d, i):
        return buf.at[col, pl.ds(d * BPS + i * CB, CB)]

    def exchange(i):
        return send(mine(i), slot(far, c, 1, i), EX + i, across)

    def near_halo(d, i):
        return send(mine(i), slot(near, c, 2 * d, i), NEAR + d * CHUNKS + i, (sides[d], g))

    def far_direct(d, i):
        return send(mine(i), slot(far, c, 2 * d, i), FAR + d * CHUNKS + i, (sides[d], other))

    def far_relay(d, i):
        return send(slot(far, c, 1, i), slot(far, c, 2 * d, i), FAR + d * CHUNKS + i, (sides[d], g))

    def to_partner(buf, d, i, sem):
        return send(slot(buf, c, d, i), slot(buf, c, d, i), sem, partner)

    own_copy = send(t_cur, near.at[c, pl.ds(BPS, BPS)], OWN, partner)

    for i in range(CHUNKS):
        exchange(i).start()
    for d in range(2):
        near_halo(d, 0).start()
    for d in range(2):
        @pl.when(edge[d])
        def _():
            for i in range(CHUNKS):
                far_direct(d, i).start()
    own_copy.start()

    for i in range(CHUNKS):
        exchange(i).wait_recv()
        for d in range(2):
            @pl.when(jnp.logical_not(edge[d]))
            def _():
                far_relay(d, i).start()
        to_partner(far, 1, i, EXC + i).start()
        if i == CHUNKS - 1:
            for d in range(2):
                for j in range(1, CHUNKS):
                    near_halo(d, j).start()
        if i < MINE:
            loads[3 + i].wait()
            relayout(x, stage, a, i, 0, 1)
            assemble(stage, a, i)

    for i in range(CHUNKS):
        for d in range(2):
            far_relay(d, i).wait_recv()
            to_partner(far, 2 * d, i, FARC + d * CHUNKS + i).start()
    for i in range(CHUNKS):
        to_partner(far, 1, i, EXC + i).wait_recv()
        for d in range(2):
            to_partner(far, 2 * d, i, FARC + d * CHUNKS + i).wait_recv()

    multiply(ids, a, far, out_far)

    def far_image(r):
        col = lax.rem(c + r, 2)
        return send(out_far.at[col], image.at[pl.ds(g * MINE, MINE)], IMG + 1 + r, here(1 - h, col))

    for r in range(2):
        far_image(r).start()

    for i in range(CHUNKS):
        for d in range(2):
            near_halo(d, i).wait_recv()
            to_partner(near, 2 * d, i, NEARC + d * CHUNKS + i).start()
    loads[0].wait()
    own_copy.wait_recv()
    for i in range(CHUNKS):
        for d in range(2):
            to_partner(near, 2 * d, i, NEARC + d * CHUNKS + i).wait_recv()

    multiply(ids, a, near, out_near)

    near_image = send(out_near.at[1 - c], image.at[pl.ds(g * MINE, MINE)], IMG, partner)
    near_image.start()

    loads[1].wait()
    loads[2].wait()

    def finish(first, source, at, sums):
        def body(b, sums):
            blk = first + b
            value = 2.0 * source[at + b] - prev[blk]
            t_next[blk] = value
            fold = lambda v: jnp.sum(v.reshape(BS // 8, 8, COLS), axis=0)
            return (
                sums[0] + fold(probe[blk] * value),
                sums[1] + fold(near[c, BPS + blk].astype(jnp.float32) * value),
            )

        return lax.fori_loop(0, MINE, body, sums)

    zero = jnp.zeros((8, COLS), jnp.float32)
    sums = finish(g * MINE, out_near.at[c], 0, (zero, zero))
    near_image.wait_recv()
    first = (h * 2 + 1 - c) * MINE
    sums = finish(first, image, first, sums)
    for r in range(2):
        far_image(r).wait_recv()
        first = ((1 - h) * 2 + lax.rem(c + r, 2)) * MINE
        sums = finish(first, image, first, sums)

    top = lax.broadcasted_iota(jnp.int32, (8, COLS), 0)
    pack = lambda p, q: jnp.where(
        top == 0, jnp.sum(p, axis=0, keepdims=True), jnp.where(top == 1, jnp.sum(q, axis=0, keepdims=True), 0.0)
    )

    def spread(buf, me, peer, sem, value):
        buf[me] = value
        copies = [send(buf.at[me], buf.at[me], sem + o, peer(o)) for o in range(1, 8)]
        for copy in copies:
            copy.start()
        for copy in copies:
            copy.wait_recv()
        total = buf[0]
        for i in range(1, 8):
            total = total + buf[i]
        return total, copies

    part, copies1 = spread(sums1, z, zpeer, M1, pack(*sums))
    whole, copies2 = spread(sums2, row, rpeer, M2, part)
    factor = 1.0 / math.sqrt(SLABS * BPS * BS)
    moments[...] = whole[0:2] * factor

    own_copy.wait_send()
    near_image.wait_send()
    for r in range(2):
        far_image(r).wait_send()
    for i in range(CHUNKS):
        exchange(i).wait_send()
        to_partner(far, 1, i, EXC + i).wait_send()
        for d in range(2):
            near_halo(d, i).wait_send()
            far_relay(d, i).wait_send()
            to_partner(far, 2 * d, i, FARC + d * CHUNKS + i).wait_send()
            to_partner(near, 2 * d, i, NEARC + d * CHUNKS + i).wait_send()
    for copy in copies1 + copies2:
        copy.wait_send()


def shards(tiles, neighbours, t_cur, t_prev, probes):
    f32, bf16 = jnp.float32, jnp.bfloat16
    anywhere = pl.BlockSpec(memory_space=pl.ANY)
    vmem = pl.BlockSpec(memory_space=pltpu.VMEM)
    return pl.pallas_call(
        kernel,
        out_shape=(
            jax.ShapeDtypeStruct((BPS, BS, COLS), f32),
            jax.ShapeDtypeStruct((2, COLS), f32),
        ),
        in_specs=[pl.BlockSpec(memory_space=pltpu.SMEM)] + [anywhere] * 4,
        out_specs=(vmem, vmem),
        scratch_shapes=[
            pltpu.VMEM((MINE, NB, BS * BS), bf16),
            pltpu.VMEM((NB * PITCH, LANES), f32),
            pltpu.VMEM((MINE, BS, KPAD), bf16),
            pltpu.VMEM((2, 3 * BPS, BS, COLS), bf16),
            pltpu.VMEM((2, 3 * BPS, BS, COLS), bf16),
            pltpu.VMEM((2, MINE, BS, COLS), f32),
            pltpu.VMEM((2, MINE, BS, COLS), f32),
            pltpu.VMEM((BPS, BS, COLS), f32),
            pltpu.VMEM((BPS, BS, COLS), f32),
            pltpu.VMEM((BPS, BS, COLS), f32),
            pltpu.SMEM((MINE * NB,), jnp.int32),
            pltpu.VMEM((8, 8, COLS), f32),
            pltpu.VMEM((8, 8, COLS), f32),
            pltpu.SemaphoreType.DMA((6,)),
            pltpu.SemaphoreType.DMA((NSEM,)),
            pltpu.SemaphoreType.DMA((NSEM,)),
        ],
        compiler_params=pltpu.CompilerParams(
            collective_id=0, has_side_effects=True, vmem_limit_bytes=60 << 20
        ),
        name="chebyshev_step",
    )(neighbours, tiles, t_cur, t_prev, probes)


def solution(mesh):
    placed = (
        P(("slab", "grp"), None, None),
        P("slab", None),
        P("slab", None, "grp"),
        P("slab", None, "grp"),
        P("slab", None, "grp"),
    )
    return jax.shard_map(
        shards,
        mesh=mesh,
        in_specs=placed,
        out_specs=(P("slab", None, "grp"), P(None, "grp")),
        check_vma=False,
    )
```

```python
import functools
import math

import jax
import jax.numpy as jnp
from jax import lax
from jax.experimental import pallas as pl
from jax.experimental.pallas import tpu as pltpu
from jax.sharding import PartitionSpec as P

MESH = pl.DeviceIdType.MESH
BPS, BS, NB = 12, 192, 27
MINE = 3
COLS = 128
LANES = 128
FLAT = BS * BS // LANES
PITCH = FLAT + 1
KPAD = 5248
CHUNKS = 6
AHEAD = 2
EARLY = 3
CB = BPS // CHUNKS
SLABS, ZS = 64, 8


class Sems:
    def __init__(self):
        self.n = 0

    def take(self, *dims):
        size = math.prod(dims) if dims else 1
        start = self.n
        self.n += size
        return start


RX = Sems()
EX, OWN, EXC = RX.take(CHUNKS), RX.take(), RX.take(CHUNKS)
NEAR, FAR, NEARC, FARC, XS = [RX.take(2, CHUNKS) for _ in range(5)]
IMG, IMGF, M1, M2 = RX.take(), RX.take(2, MINE), RX.take(8), RX.take(8)
NSEM = RX.n


def relayout(x, stage, b):
    step = 12

    def spread(m, carry):
        for u in range(step):
            j = m * step + u
            v = x[b, :, pl.ds(pl.multiple_of(j * LANES, LANES), LANES)]
            stage[pl.ds(j, NB, stride=PITCH), :] = v.astype(jnp.float32)
        return carry

    lax.fori_loop(0, FLAT // step, spread, 0)


def assemble(stage, a, b):
    low = lax.broadcasted_iota(jnp.int32, (BS // 2, LANES), 1) < 64
    load = lambda k, i: stage[pl.ds(k * PITCH + i, BS // 2, stride=3), :]
    turn = lambda v: pltpu.roll(v, 64, 1)

    def pair(p, last):
        k = 2 * p
        e0, e1, e2 = [load(k, i) for i in range(3)]
        if last:
            zero = jnp.zeros_like(e0)
            f1, f2, rf0, rf1 = zero, zero, zero, zero
        else:
            f0, f1, f2 = [load(k + 1, i) for i in range(3)]
            rf0, rf1 = turn(f0), turn(f1)
        re1, re2 = turn(e1), turn(e2)
        even = [e0, jnp.where(low, e1, rf0), jnp.where(low, rf0, rf1)]
        odd = [jnp.where(low, re1, re2), jnp.where(low, re2, f1), f2]
        for t in range(2 if last else 3):
            at = pl.ds(pl.multiple_of(p * 384 + 128 * t, 128), LANES)
            a[b, 0 : BS // 2, at] = even[t].astype(jnp.bfloat16)
            a[b, BS // 2 : BS, at] = odd[t].astype(jnp.bfloat16)

    def body(p, carry):
        pair(p, False)
        return carry

    lax.fori_loop(0, NB // 2, body, 0)
    pair(NB // 2, True)


def multiply(ids, a, near, out, after=None):
    def one(b, carry):
        def rhs(k):
            n = ids[b * NB + k]
            return jnp.concatenate([near[0, n], near[1, n]], axis=1)

        total = None
        for first in range(0, NB, 4):
            ks = range(first, min(first + 4, NB))
            parts = [rhs(k) for k in ks]
            if len(parts) == 3:
                parts.append(jnp.zeros((64, 2 * COLS), jnp.bfloat16))
            right = jnp.concatenate(parts, axis=0)
            left = a[b, :, first * BS : first * BS + right.shape[0]]
            term = jnp.dot(left, right, preferred_element_type=jnp.float32)
            total = term if total is None else total + term
        half = BS // 2
        for e in range(2):
            for c in range(2):
                out[c, b, pl.ds(e, half, stride=2), :] = total[
                    half * e : half * (e + 1), COLS * c : COLS * (c + 1)
                ]
        if after is not None:
            after(b)
        return carry

    lax.fori_loop(0, MINE, one, 0)


def kernel(
    neighbours, tiles, t_cur, t_prev, probes, t_next, moments,
    x, stage, a, near, far, out_far, out_near, image, passing, prev, probe, ids, sums1, sums2,
    local, ssem, rsem,
):
    s, g = lax.axis_index("slab"), lax.axis_index("grp")
    z = lax.rem(s, ZS)
    row = lax.div(s, ZS)
    h, c = lax.div(g, 2), lax.rem(g, 2)
    up, down = lax.rem(s + 1, SLABS), lax.rem(s + SLABS - 1, SLABS)
    here = lambda hh, cc: (s, hh * 2 + cc)
    partner, across, cross = here(h, 1 - c), here(1 - h, c), here(1 - h, 1 - c)
    zpeer = lambda o: (row * ZS + lax.rem(z + o, ZS), g)
    rpeer = lambda o: (lax.rem(row + o, 8) * ZS + z, g)
    other = (1 - h) * 2 + c
    beside = lambda slab: slab + ZS - 2 * ZS * lax.rem(lax.div(slab, ZS), 2)
    sx = beside(s)
    xpeer = ((sx, g), (sx, other))
    sides = (up, down)
    edge = (z == ZS - 1, z == 0)
    on_edge = jnp.logical_or(edge[0], edge[1])
    inner = [jnp.logical_not(e) for e in edge]
    de = jnp.where(edge[1], 1, 0)
    beyond = (lax.rem(jnp.where(edge[1], sx + SLABS - 1, sx + 1), SLABS), g)
    greet = [(jnp.where(edge[d], beside(sides[d]), sides[d]), g) for d in range(2)]

    loads = [
        pltpu.make_async_copy(t_cur, near.at[c, pl.ds(BPS, BPS)], local.at[0]),
        pltpu.make_async_copy(t_prev, prev, local.at[1]),
        pltpu.make_async_copy(probes, probe, local.at[2]),
    ] + [pltpu.make_async_copy(tiles.at[b], x.at[b], local.at[3 + b]) for b in range(MINE)]

    barrier = pltpu.get_barrier_semaphore()
    peers = [partner, across, cross]
    peers += greet + list(xpeer)
    peers += [zpeer(o) for o in range(1, ZS)] + [rpeer(o) for o in range(1, 8)]
    for peer in peers:
        pl.semaphore_signal(barrier, 1, device_id=peer, device_id_type=MESH)
    for load in loads:
        load.start()

    def indices(b, carry):
        for k in range(NB):
            n = neighbours[g * MINE + b, k]
            rel = lax.rem(lax.div(n, BPS) - s + 1 + SLABS, SLABS)
            ids[b * NB + k] = jnp.minimum(rel, 2) * BPS + lax.rem(n, BPS)
        return carry

    lax.fori_loop(0, MINE, indices, 0)
    pl.semaphore_wait(barrier, len(peers))

    def send(src, dst, sem, device):
        return pltpu.make_async_remote_copy(
            src, dst, ssem.at[sem], rsem.at[sem], device_id=device, device_id_type=MESH
        )

    def mine(i):
        return t_cur.at[pl.ds(i * CB, CB)]

    def slot(buf, col, d, i):
        return buf.at[col, pl.ds(d * BPS + i * CB, CB)]

    def exchange(i):
        return send(mine(i), slot(far, c, 1, i), EX + i, across)

    def near_halo(d, i):
        return send(mine(i), slot(near, c, 2 * d, i), NEAR + d * CHUNKS + i, (sides[d], g))

    def chunk(e, i):
        return passing.at[e, pl.ds(i * CB, CB)]

    def hand(e, i):
        return send(mine(i), chunk(e, i), XS + e * CHUNKS + i, xpeer[e])

    def forward(e, i):
        base = (NEAR, FAR)[e] + de * CHUNKS + i
        return send(chunk(e, i), slot((near, far)[e], c, 2 * de, i), base, beyond)

    def forward_across(i):
        return send(chunk(i % 2, i), slot(far, c, 1, i), EX + i, xpeer[1 - i % 2])

    def far_relay(d, i):
        return send(slot(far, c, 1, i), slot(far, c, 2 * d, i), FAR + d * CHUNKS + i, (sides[d], g))

    def to_partner(buf, d, i, sem):
        return send(slot(buf, c, d, i), slot(buf, c, d, i), sem, partner)

    own_copy = send(t_cur, near.at[c, pl.ds(BPS, BPS)], OWN, partner)

    @pl.when(on_edge)
    def _():
        for i in range(AHEAD):
            for e in range(2):
                hand(e, i).start()

    @pl.when(jnp.logical_not(on_edge))
    def _():
        for i in range(CHUNKS):
            exchange(i).start()

    for d in range(2):
        @pl.when(inner[d])
        def _():
            for i in range(EARLY):
                near_halo(d, i).start()
    own_copy.start()

    for i in range(CHUNKS + 1):
        if i < CHUNKS:
            @pl.when(on_edge)
            def _():
                for e in range(2):
                    hand(e, i).wait_recv()
                forward_across(i).start()
                for e in range(2):
                    if i + AHEAD < CHUNKS:
                        hand(e, i + AHEAD).start()
                    forward(e, i).start()

        if i > 0:
            j = i - 1
            exchange(j).wait_recv()
            for d in range(2):
                @pl.when(inner[d])
                def _():
                    far_relay(d, j).start()
                    if j == CHUNKS - 1:
                        for k in range(EARLY, CHUNKS):
                            near_halo(d, k).start()
            to_partner(far, 1, j, EXC + j).start()
            if j < MINE:
                loads[3 + j].wait()
                relayout(x, stage, j)
                assemble(stage, a, j)

    for i in range(CHUNKS):
        for d in range(2):
            far_relay(d, i).wait_recv()
            to_partner(far, 2 * d, i, FARC + d * CHUNKS + i).start()
    for i in range(CHUNKS):
        to_partner(far, 1, i, EXC + i).wait_recv()
        for d in range(2):
            to_partner(far, 2 * d, i, FARC + d * CHUNKS + i).wait_recv()

    def far_image(r, b):
        col = lax.rem(c + r, 2)
        sem = IMGF + r * MINE + b
        return send(out_far.at[col, b], image.at[g * MINE + b], sem, here(1 - h, col))

    def send_far(b):
        for r in range(2):
            far_image(r, b).start()

    multiply(ids, a, far, out_far, send_far)

    for i in range(CHUNKS):
        for d in range(2):
            near_halo(d, i).wait_recv()
            to_partner(near, 2 * d, i, NEARC + d * CHUNKS + i).start()
    loads[0].wait()
    own_copy.wait_recv()
    for i in range(CHUNKS):
        for d in range(2):
            to_partner(near, 2 * d, i, NEARC + d * CHUNKS + i).wait_recv()

    multiply(ids, a, near, out_near)

    near_image = send(out_near.at[1 - c], image.at[pl.ds(g * MINE, MINE)], IMG, partner)
    near_image.start()

    loads[1].wait()
    loads[2].wait()

    def finish(first, source, at):
        def body(b, sums):
            blk = first + b
            value = 2.0 * source[at + b] - prev[blk]
            t_next[blk] = value
            fold = lambda v: jnp.sum(v.reshape(BS // 8, 8, COLS), axis=0)
            return (
                sums[0] + fold(probe[blk] * value),
                sums[1] + fold(near[c, BPS + blk].astype(jnp.float32) * value),
            )

        return body

    def finish_all(first, source, at, sums):
        return lax.fori_loop(0, MINE, finish(first, source, at), sums)

    zero = jnp.zeros((8, COLS), jnp.float32)
    sums = finish_all(g * MINE, out_near.at[c], 0, (zero, zero))
    near_image.wait_recv()
    first = (h * 2 + 1 - c) * MINE
    sums = finish_all(first, image, first, sums)

    def arrived(b, sums):
        for r in range(2):
            far_image(r, b).wait_recv()
            first = ((1 - h) * 2 + lax.rem(c + r, 2)) * MINE
            sums = finish(first, image, first)(b, sums)
        return sums

    sums = lax.fori_loop(0, MINE, arrived, sums)

    top = lax.broadcasted_iota(jnp.int32, (8, COLS), 0)
    pack = lambda p, q: jnp.where(
        top == 0, jnp.sum(p, axis=0, keepdims=True), jnp.where(top == 1, jnp.sum(q, axis=0, keepdims=True), 0.0)
    )

    def spread(buf, me, peer, sem, value):
        buf[me] = value
        copies = [send(buf.at[me], buf.at[me], sem + o, peer(o)) for o in range(1, 8)]
        for copy in copies:
            copy.start()
        for copy in copies:
            copy.wait_recv()
        total = buf[0]
        for i in range(1, 8):
            total = total + buf[i]
        return total, copies

    part, copies1 = spread(sums1, z, zpeer, M1, pack(*sums))
    whole, copies2 = spread(sums2, row, rpeer, M2, part)
    factor = 1.0 / math.sqrt(SLABS * BPS * BS)
    moments[...] = whole[0:2] * factor

    own_copy.wait_send()
    near_image.wait_send()
    for r in range(2):
        for b in range(MINE):
            far_image(r, b).wait_send()
    for i in range(CHUNKS):
        @pl.when(on_edge)
        def _():
            for e in range(2):
                hand(e, i).wait_send()
                forward(e, i).wait_send()
            forward_across(i).wait_send()

        @pl.when(jnp.logical_not(on_edge))
        def _():
            exchange(i).wait_send()

        to_partner(far, 1, i, EXC + i).wait_send()
        for d in range(2):
            @pl.when(inner[d])
            def _():
                near_halo(d, i).wait_send()
                far_relay(d, i).wait_send()

            to_partner(far, 2 * d, i, FARC + d * CHUNKS + i).wait_send()
            to_partner(near, 2 * d, i, NEARC + d * CHUNKS + i).wait_send()
    for copy in copies1 + copies2:
        copy.wait_send()


def shards(tiles, neighbours, t_cur, t_prev, probes):
    f32, bf16 = jnp.float32, jnp.bfloat16
    anywhere = pl.BlockSpec(memory_space=pl.ANY)
    vmem = pl.BlockSpec(memory_space=pltpu.VMEM)
    return pl.pallas_call(
        kernel,
        out_shape=(
            jax.ShapeDtypeStruct((BPS, BS, COLS), f32),
            jax.ShapeDtypeStruct((2, COLS), f32),
        ),
        in_specs=[pl.BlockSpec(memory_space=pltpu.SMEM)] + [anywhere] * 4,
        out_specs=(vmem, vmem),
        scratch_shapes=[
            pltpu.VMEM((MINE, NB, BS * BS), bf16),
            pltpu.VMEM((NB * PITCH, LANES), f32),
            pltpu.VMEM((MINE, BS, KPAD), bf16),
            pltpu.VMEM((2, 3 * BPS, BS, COLS), bf16),
            pltpu.VMEM((2, 3 * BPS, BS, COLS), bf16),
            pltpu.VMEM((2, MINE, BS, COLS), f32),
            pltpu.VMEM((2, MINE, BS, COLS), f32),
            pltpu.VMEM((BPS, BS, COLS), f32),
            pltpu.VMEM((2, BPS, BS, COLS), bf16),
            pltpu.VMEM((BPS, BS, COLS), f32),
            pltpu.VMEM((BPS, BS, COLS), f32),
            pltpu.SMEM((MINE * NB,), jnp.int32),
            pltpu.VMEM((8, 8, COLS), f32),
            pltpu.VMEM((8, 8, COLS), f32),
            pltpu.SemaphoreType.DMA((6,)),
            pltpu.SemaphoreType.DMA((NSEM,)),
            pltpu.SemaphoreType.DMA((NSEM,)),
        ],
        compiler_params=pltpu.CompilerParams(
            collective_id=0, has_side_effects=True, vmem_limit_bytes=60 << 20
        ),
        name="chebyshev_step",
    )(neighbours, tiles, t_cur, t_prev, probes)


def solution(mesh):
    placed = (
        P(("slab", "grp"), None, None),
        P("slab", None),
        P("slab", None, "grp"),
        P("slab", None, "grp"),
        P("slab", None, "grp"),
    )
    return jax.shard_map(
        shards,
        mesh=mesh,
        in_specs=placed,
        out_specs=(P("slab", None, "grp"), P(None, "grp")),
        check_vma=False,
    )
```

```python
import functools
import math

import jax
import jax.numpy as jnp
from jax import lax
from jax.experimental import pallas as pl
from jax.experimental.pallas import tpu as pltpu
from jax.sharding import PartitionSpec as P

MESH = pl.DeviceIdType.MESH
BPS, BS, NB = 12, 192, 27
MINE = 3
COLS = 128
LANES = 128
FLAT = BS * BS // LANES
PITCH = FLAT + 1
KPAD = 5248
CHUNKS = 6
LAG = 2
AHEAD = 3
EARLY = 3
HALF = CHUNKS // 2
CB = BPS // CHUNKS
SLABS, ZS = 64, 8


class Sems:
    def __init__(self):
        self.n = 0

    def take(self, *dims):
        size = math.prod(dims) if dims else 1
        start = self.n
        self.n += size
        return start


RX = Sems()
EX, OWN, EXC = RX.take(CHUNKS), RX.take(2), RX.take(CHUNKS)
NEAR, FAR, NEARC, FARC, XS = [RX.take(2, CHUNKS) for _ in range(5)]
IMG, IMGF, M1, M2 = RX.take(MINE), RX.take(2, MINE), RX.take(8), RX.take(8)
NSEM = RX.n


def relayout(x, stage, b):
    step = 12

    def spread(m, carry):
        for u in range(step):
            j = m * step + u
            v = x[b, :, pl.ds(pl.multiple_of(j * LANES, LANES), LANES)]
            stage[pl.ds(j, NB, stride=PITCH), :] = v.astype(jnp.float32)
        return carry

    lax.fori_loop(0, FLAT // step, spread, 0)


def assemble(stage, a, b):
    low = lax.broadcasted_iota(jnp.int32, (BS // 2, LANES), 1) < 64
    load = lambda k, i: stage[pl.ds(k * PITCH + i, BS // 2, stride=3), :]
    turn = lambda v: pltpu.roll(v, 64, 1)

    def pair(p, last):
        k = 2 * p
        e0, e1, e2 = [load(k, i) for i in range(3)]
        if last:
            zero = jnp.zeros_like(e0)
            f1, f2, rf0, rf1 = zero, zero, zero, zero
        else:
            f0, f1, f2 = [load(k + 1, i) for i in range(3)]
            rf0, rf1 = turn(f0), turn(f1)
        re1, re2 = turn(e1), turn(e2)
        even = [e0, jnp.where(low, e1, rf0), jnp.where(low, rf0, rf1)]
        odd = [jnp.where(low, re1, re2), jnp.where(low, re2, f1), f2]
        for t in range(2 if last else 3):
            at = pl.ds(pl.multiple_of(p * 384 + 128 * t, 128), LANES)
            a[b, 0 : BS // 2, at] = even[t].astype(jnp.bfloat16)
            a[b, BS // 2 : BS, at] = odd[t].astype(jnp.bfloat16)

    def body(p, carry):
        pair(p, False)
        return carry

    lax.fori_loop(0, NB // 2, body, 0)
    pair(NB // 2, True)


def multiply(ids, a, col, out, after):
    def one(b, carry):
        total = None
        for first in range(0, NB, 4):
            parts = [col[ids[b * NB + k]] for k in range(first, min(first + 4, NB))]
            if len(parts) == 3:
                parts.append(jnp.zeros((64, COLS), jnp.bfloat16))
            right = jnp.concatenate(parts, axis=0)
            left = a[b, :, first * BS : first * BS + right.shape[0]]
            term = jnp.dot(left, right, preferred_element_type=jnp.float32)
            total = term if total is None else total + term
        half = BS // 2
        for e in range(2):
            out[b, pl.ds(e, half, stride=2), :] = total[half * e : half * (e + 1)]
        after(b)
        return carry

    lax.fori_loop(0, MINE, one, 0)


def kernel(
    table, tiles, t_cur, t_prev, probes, t_next, moments,
    x, stage, a, near0, near1, far0, far1, own, out_far, out_near, image, passing, prev, probe, neighbours, ids, sums1, sums2,
    local, ssem, rsem,
):
    near, far = (near0, near1), (far0, far1)
    s, g = lax.axis_index("slab"), lax.axis_index("grp")
    z = lax.rem(s, ZS)
    row = lax.div(s, ZS)
    h, c = lax.div(g, 2), lax.rem(g, 2)
    up, down = lax.rem(s + 1, SLABS), lax.rem(s + SLABS - 1, SLABS)
    here = lambda hh, cc: (s, hh * 2 + cc)
    partner, across, cross = here(h, 1 - c), here(1 - h, c), here(1 - h, 1 - c)
    zpeer = lambda o: (row * ZS + lax.rem(z + o, ZS), g)
    rpeer = lambda o: (lax.rem(row + o, 8) * ZS + z, g)
    other = (1 - h) * 2 + c
    beside = lambda slab: slab + ZS - 2 * ZS * lax.rem(lax.div(slab, ZS), 2)
    sx = beside(s)
    xpeer = ((sx, g), (sx, other))
    sides = (up, down)
    edge = (z == ZS - 1, z == 0)
    on_edge = jnp.logical_or(edge[0], edge[1])
    inner = [jnp.logical_not(e) for e in edge]
    de = jnp.where(edge[1], 1, 0)
    beyond = (lax.rem(jnp.where(edge[1], sx + SLABS - 1, sx + 1), SLABS), g)
    greet = [(jnp.where(edge[d], beside(sides[d]), sides[d]), g) for d in range(2)]

    loads = [
        pltpu.make_async_copy(t_cur, own, local.at[0]),
        pltpu.make_async_copy(t_prev, prev, local.at[1]),
        pltpu.make_async_copy(probes, probe, local.at[2]),
    ] + [pltpu.make_async_copy(tiles.at[b], x.at[b], local.at[3 + b]) for b in range(MINE)]
    loads.append(pltpu.make_async_copy(table, neighbours, local.at[3 + MINE]))

    barrier = pltpu.get_barrier_semaphore()
    peers = [partner, across, cross]
    peers += greet + list(xpeer)
    peers += [zpeer(o) for o in range(1, ZS)] + [rpeer(o) for o in range(1, 8)]
    for peer in peers:
        pl.semaphore_signal(barrier, 1, device_id=peer, device_id_type=MESH)
    def place_own(k):
        return pltpu.make_async_copy(t_cur, near[k].at[pl.ds(BPS, BPS)], local.at[4 + MINE])

    for k in range(2):
        @pl.when(c == k)
        def _():
            place_own(k).start()

    for load in loads:
        load.start()

    def indices(b, carry):
        for k in range(NB):
            n = neighbours[g * MINE + b, k]
            rel = lax.rem(lax.div(n, BPS) - s + 1 + SLABS, SLABS)
            ids[b * NB + k] = jnp.minimum(rel, 2) * BPS + lax.rem(n, BPS)
        return carry

    pl.semaphore_wait(barrier, len(peers))

    def send(src, dst, sem, device):
        return pltpu.make_async_remote_copy(
            src, dst, ssem.at[sem], rsem.at[sem], device_id=device, device_id_type=MESH
        )

    def slot(buf, d, i):
        return buf[i // HALF].at[pl.ds(d * BPS + c * (BPS // 2) + (i % HALF) * CB, CB)]

    def mine(i):
        return slot(near, 1, i)

    def exchange(i):
        return send(mine(i), slot(far, 1, i), EX + i, across)

    def near_halo(d, i):
        return send(mine(i), slot(near, 2 * d, i), NEAR + d * CHUNKS + i, (sides[d], g))

    def chunk(e, i):
        return passing.at[e, pl.ds(i * CB, CB)]

    def hand(e, i):
        return send(mine(i), chunk(e, i), XS + e * CHUNKS + i, xpeer[e])

    def forward(e, i):
        base = (NEAR, FAR)[e] + de * CHUNKS + i
        return send(chunk(e, i), slot((near, far)[e], 2 * de, i), base, beyond)

    def forward_across(i):
        return send(chunk(i % 2, i), slot(far, 1, i), EX + i, xpeer[1 - i % 2])

    def far_relay(d, i):
        return send(slot(far, 1, i), slot(far, 2 * d, i), FAR + d * CHUNKS + i, (sides[d], g))

    def to_partner(buf, d, i, sem):
        return send(slot(buf, d, i), slot(buf, d, i), sem, partner)

    def own_copy(p, k=0):
        first = BPS + (BPS // 2) * (1 - c if p == 0 else c)
        piece = near[k].at[pl.ds(first, BPS // 2)]
        return send(piece, piece, OWN + p, partner)

    place_own(0).wait()
    for k in range(2):
        @pl.when(c == k)
        def _():
            for p in range(2):
                own_copy(p, k).start()

    @pl.when(c == 1)
    def _():
        own_copy(0).wait_recv()

    def begin(chunks):
        @pl.when(jnp.logical_not(on_edge))
        def _():
            for i in chunks:
                exchange(i).start()

    @pl.when(on_edge)
    def _():
        for i in range(AHEAD):
            for e in range(2):
                hand(e, i).start()

    begin(range(HALF))
    for d in range(2):
        @pl.when(inner[d])
        def _():
            for i in range(EARLY):
                near_halo(d, i).start()

    @pl.when(c == 0)
    def _():
        own_copy(0).wait_recv()

    begin(range(HALF, CHUNKS))
    loads[3 + MINE].wait()
    lax.fori_loop(0, MINE, indices, 0)

    def prepare(b):
        loads[3 + b].wait()
        relayout(x, stage, b)
        assemble(stage, a, b)


    def far_forward(col):
        for i in range(col * HALF, (col + 1) * HALF):
            for d in range(2):
                far_relay(d, i).wait_recv()
                to_partner(far, 2 * d, i, FARC + d * CHUNKS + i).start()

    def far_image(col, b):
        r = jnp.where(col == c, 0, 1)
        return send(out_far.at[col, b], image.at[g * MINE + b], IMGF + r * MINE + b, here(1 - h, col))

    def far_multiply(col):
        for i in range(col * HALF, (col + 1) * HALF):
            to_partner(far, 1, i, EXC + i).wait_recv()
            for d in range(2):
                to_partner(far, 2 * d, i, FARC + d * CHUNKS + i).wait_recv()
        multiply(ids, a, far[col], out_far.at[col], lambda b: far_image(col, b).start())

    for i in range(CHUNKS + LAG):
        if i < CHUNKS:
            @pl.when(on_edge)
            def _():
                for e in range(2):
                    hand(e, i).wait_recv()
                forward_across(i).start()
                for e in range(2):
                    if i + AHEAD < CHUNKS:
                        hand(e, i + AHEAD).start()
                    forward(e, i).start()

        if i >= LAG:
            j = i - LAG
            exchange(j).wait_recv()
            for d in range(2):
                @pl.when(inner[d])
                def _():
                    far_relay(d, j).start()
                    @pl.when(on_edge)
                    def _():
                        if j + EARLY < CHUNKS:
                            near_halo(d, j + EARLY).start()

                    if j == CHUNKS - 1:
                        @pl.when(jnp.logical_not(on_edge))
                        def _():
                            for k in range(EARLY, CHUNKS):
                                near_halo(d, k).start()
            to_partner(far, 1, j, EXC + j).start()
            if j < MINE:
                prepare(j)
            if j == CHUNKS - 2:
                far_forward(0)

    far_multiply(0)
    far_forward(1)
    far_multiply(1)

    def near_image(b):
        return send(out_near.at[1 - c, b], image.at[g * MINE + b], IMG + b, partner)

    own_copy(1).wait_recv()
    for col in range(2):
        for i in range(col * HALF, (col + 1) * HALF):
            for d in range(2):
                near_halo(d, i).wait_recv()
                to_partner(near, 2 * d, i, NEARC + d * CHUNKS + i).start()
        for i in range(col * HALF, (col + 1) * HALF):
            for d in range(2):
                to_partner(near, 2 * d, i, NEARC + d * CHUNKS + i).wait_recv()

        def after(b):
            @pl.when(c != col)
            def _():
                near_image(b).start()

        multiply(ids, a, near[col], out_near.at[col], after)

    for k in range(3):
        loads[k].wait()

    def finish(first, source, at):
        def body(b, sums):
            blk = first + b
            value = 2.0 * source[at + b] - prev[blk]
            t_next[blk] = value
            fold = lambda v: jnp.sum(v.reshape(BS // 8, 8, COLS), axis=0)
            return (
                sums[0] + fold(probe[blk] * value),
                sums[1] + fold(own[blk].astype(jnp.float32) * value),
            )

        return body

    def finish_all(first, source, at, sums):
        return lax.fori_loop(0, MINE, finish(first, source, at), sums)

    zero = jnp.zeros((8, COLS), jnp.float32)
    sums = finish_all(g * MINE, out_near.at[c], 0, (zero, zero))
    first = (h * 2 + 1 - c) * MINE
    for b in range(MINE):
        near_image(b).wait_recv()
    sums = finish_all(first, image, first, sums)

    def arrived(b, sums):
        for r in range(2):
            send(out_far.at[0, b], image.at[b], IMGF + r * MINE + b, across).wait_recv()
            first = ((1 - h) * 2 + (c if r == 0 else 1 - c)) * MINE
            sums = finish(first, image, first)(b, sums)
        return sums

    sums = lax.fori_loop(0, MINE, arrived, sums)

    top = lax.broadcasted_iota(jnp.int32, (8, COLS), 0)
    pack = lambda p, q: jnp.where(
        top == 0, jnp.sum(p, axis=0, keepdims=True), jnp.where(top == 1, jnp.sum(q, axis=0, keepdims=True), 0.0)
    )

    def spread(buf, me, peer, sem, value):
        buf[me] = value
        copies = [send(buf.at[me], buf.at[me], sem + o, peer(o)) for o in range(1, 8)]
        for copy in copies:
            copy.start()
        for copy in copies:
            copy.wait_recv()
        total = buf[0]
        for i in range(1, 8):
            total = total + buf[i]
        return total, copies

    part, copies1 = spread(sums1, z, zpeer, M1, pack(*sums))
    whole, copies2 = spread(sums2, row, rpeer, M2, part)
    factor = 1.0 / math.sqrt(SLABS * BPS * BS)
    moments[...] = whole[0:2] * factor

    for p in range(2):
        own_copy(p).wait_send()
    for b in range(MINE):
        near_image(b).wait_send()
        for col in range(2):
            far_image(col, b).wait_send()
    for i in range(CHUNKS):
        @pl.when(on_edge)
        def _():
            for e in range(2):
                hand(e, i).wait_send()
                forward(e, i).wait_send()
            forward_across(i).wait_send()

        @pl.when(jnp.logical_not(on_edge))
        def _():
            exchange(i).wait_send()

        to_partner(far, 1, i, EXC + i).wait_send()
        for d in range(2):
            @pl.when(inner[d])
            def _():
                near_halo(d, i).wait_send()
                far_relay(d, i).wait_send()

            to_partner(far, 2 * d, i, FARC + d * CHUNKS + i).wait_send()
            to_partner(near, 2 * d, i, NEARC + d * CHUNKS + i).wait_send()
    for copy in copies1 + copies2:
        copy.wait_send()


def shards(tiles, neighbours, t_cur, t_prev, probes):
    f32, bf16 = jnp.float32, jnp.bfloat16
    anywhere = pl.BlockSpec(memory_space=pl.ANY)
    vmem = pl.BlockSpec(memory_space=pltpu.VMEM)
    return pl.pallas_call(
        kernel,
        out_shape=(
            jax.ShapeDtypeStruct((BPS, BS, COLS), f32),
            jax.ShapeDtypeStruct((2, COLS), f32),
        ),
        in_specs=[anywhere] * 5,
        out_specs=(vmem, vmem),
        scratch_shapes=[
            pltpu.VMEM((MINE, NB, BS * BS), bf16),
            pltpu.VMEM((NB * PITCH, LANES), f32),
            pltpu.VMEM((MINE, BS, KPAD), bf16),
            *[pltpu.VMEM((3 * BPS, BS, COLS), bf16)] * 4,
            pltpu.VMEM((BPS, BS, COLS), bf16),
            pltpu.VMEM((2, MINE, BS, COLS), f32),
            pltpu.VMEM((2, MINE, BS, COLS), f32),
            pltpu.VMEM((BPS, BS, COLS), f32),
            pltpu.VMEM((2, BPS, BS, COLS), bf16),
            pltpu.VMEM((BPS, BS, COLS), f32),
            pltpu.VMEM((BPS, BS, COLS), f32),
            pltpu.SMEM((BPS, NB), jnp.int32),
            pltpu.SMEM((MINE * NB,), jnp.int32),
            pltpu.VMEM((8, 8, COLS), f32),
            pltpu.VMEM((8, 8, COLS), f32),
            pltpu.SemaphoreType.DMA((5 + MINE,)),
            pltpu.SemaphoreType.DMA((NSEM,)),
            pltpu.SemaphoreType.DMA((NSEM,)),
        ],
        compiler_params=pltpu.CompilerParams(
            collective_id=0, has_side_effects=True, vmem_limit_bytes=60 << 20
        ),
        name="chebyshev_step",
    )(neighbours, tiles, t_cur, t_prev, probes)


def solution(mesh):
    placed = (
        P(("slab", "grp"), None, None),
        P("slab", None),
        P("slab", None, "grp"),
        P("slab", None, "grp"),
        P("slab", None, "grp"),
    )
    return jax.shard_map(
        shards,
        mesh=mesh,
        in_specs=placed,
        out_specs=(P("slab", None, "grp"), P(None, "grp")),
        check_vma=False,
    )
```

```python
import functools
import math

import jax
import jax.numpy as jnp
from jax import lax
from jax.experimental import pallas as pl
from jax.experimental.pallas import tpu as pltpu
from jax.sharding import PartitionSpec as P

MESH = pl.DeviceIdType.MESH
BPS, BS, NB = 12, 192, 27
MINE = 3
COLS = 128
LANES = 128
FLAT = BS * BS // LANES
PITCH = FLAT + 1
KPAD = 5248
CHUNKS = 6
LAG = 2
AHEAD = 3
EARLY = 3
HALF = CHUNKS // 2
CB = BPS // CHUNKS
SLABS, ZS = 64, 8


class Sems:
    def __init__(self):
        self.n = 0

    def take(self, *dims):
        size = math.prod(dims) if dims else 1
        start = self.n
        self.n += size
        return start


RX = Sems()
EX, OWN, EXC = RX.take(CHUNKS), RX.take(2), RX.take(CHUNKS)
NEAR, FAR, NEARC, FARC, XS = [RX.take(2, CHUNKS) for _ in range(5)]
IMG, IMGF, M1, M2 = RX.take(MINE), RX.take(2, MINE), RX.take(8), RX.take(8)
NSEM = RX.n


def relayout(x, stage, b):
    step = 12

    def spread(m, carry):
        for u in range(step):
            j = m * step + u
            v = x[b, :, pl.ds(pl.multiple_of(j * LANES, LANES), LANES)]
            stage[pl.ds(j, NB, stride=PITCH), :] = v.astype(jnp.float32)
        return carry

    lax.fori_loop(0, FLAT // step, spread, 0)


def assemble(stage, a, b):
    low = lax.broadcasted_iota(jnp.int32, (BS // 2, LANES), 1) < 64
    load = lambda k, i: stage[pl.ds(k * PITCH + i, BS // 2, stride=3), :]
    turn = lambda v: pltpu.roll(v, 64, 1)

    def pair(p, last):
        k = 2 * p
        e0, e1, e2 = [load(k, i) for i in range(3)]
        if last:
            zero = jnp.zeros_like(e0)
            f1, f2, rf0, rf1 = zero, zero, zero, zero
        else:
            f0, f1, f2 = [load(k + 1, i) for i in range(3)]
            rf0, rf1 = turn(f0), turn(f1)
        re1, re2 = turn(e1), turn(e2)
        even = [e0, jnp.where(low, e1, rf0), jnp.where(low, rf0, rf1)]
        odd = [jnp.where(low, re1, re2), jnp.where(low, re2, f1), f2]
        for t in range(2 if last else 3):
            at = pl.ds(pl.multiple_of(p * 384 + 128 * t, 128), LANES)
            a[b, 0 : BS // 2, at] = even[t].astype(jnp.bfloat16)
            a[b, BS // 2 : BS, at] = odd[t].astype(jnp.bfloat16)

    def body(p, carry):
        pair(p, False)
        return carry

    lax.fori_loop(0, NB // 2, body, 0)
    pair(NB // 2, True)


def multiply(ids, a, col, out, after):
    def one(b, carry):
        total = None
        for first in range(0, NB, 4):
            parts = [col[ids[b * NB + k]] for k in range(first, min(first + 4, NB))]
            if len(parts) == 3:
                parts.append(jnp.zeros((64, COLS), jnp.bfloat16))
            right = jnp.concatenate(parts, axis=0)
            left = a[b, :, first * BS : first * BS + right.shape[0]]
            term = jnp.dot(left, right, preferred_element_type=jnp.float32)
            total = term if total is None else total + term
        half = BS // 2
        for e in range(2):
            out[b, pl.ds(e, half, stride=2), :] = total[half * e : half * (e + 1)]
        after(b)
        return carry

    lax.fori_loop(0, MINE, one, 0)


def kernel(
    table, tiles, t_cur, t_prev, probes, t_next, moments,
    x, stage, a, near0, near1, far0, far1, own, out_far, out_near, image, passing, prev, probe, neighbours, ids, sums1, sums2,
    local, ssem, rsem,
):
    near, far = (near0, near1), (far0, far1)
    s, g = lax.axis_index("slab"), lax.axis_index("grp")
    z = lax.rem(s, ZS)
    row = lax.div(s, ZS)
    h, c = lax.div(g, 2), lax.rem(g, 2)
    up, down = lax.rem(s + 1, SLABS), lax.rem(s + SLABS - 1, SLABS)
    here = lambda hh, cc: (s, hh * 2 + cc)
    partner, across, cross = here(h, 1 - c), here(1 - h, c), here(1 - h, 1 - c)
    zpeer = lambda o: (row * ZS + lax.rem(z + o, ZS), g)
    rpeer = lambda o: (lax.rem(row + o, 8) * ZS + z, g)
    other = (1 - h) * 2 + c
    beside = lambda slab: slab + ZS - 2 * ZS * lax.rem(lax.div(slab, ZS), 2)
    sx = beside(s)
    xpeer = ((sx, g), (sx, other))
    sides = (up, down)
    edge = (z == ZS - 1, z == 0)
    on_edge = jnp.logical_or(edge[0], edge[1])
    inner = [jnp.logical_not(e) for e in edge]
    de = jnp.where(edge[1], 1, 0)
    beyond = (lax.rem(jnp.where(edge[1], sx + SLABS - 1, sx + 1), SLABS), g)
    greet = [(jnp.where(edge[d], beside(sides[d]), sides[d]), g) for d in range(2)]

    loads = [
        pltpu.make_async_copy(t_cur, own, local.at[0]),
        pltpu.make_async_copy(t_prev, prev, local.at[1]),
        pltpu.make_async_copy(probes, probe, local.at[2]),
    ] + [pltpu.make_async_copy(tiles.at[b], x.at[b], local.at[3 + b]) for b in range(MINE)]
    loads.append(pltpu.make_async_copy(table, neighbours, local.at[3 + MINE]))

    barrier = pltpu.get_barrier_semaphore()
    peers = [partner, across, cross]
    peers += greet + list(xpeer)
    peers += [zpeer(o) for o in range(1, ZS)] + [rpeer(o) for o in range(1, 8)]
    for peer in peers:
        pl.semaphore_signal(barrier, 1, device_id=peer, device_id_type=MESH)
    def place_own(k):
        return pltpu.make_async_copy(t_cur, near[k].at[pl.ds(BPS, BPS)], local.at[4 + MINE])

    for k in range(2):
        @pl.when(c == k)
        def _():
            place_own(k).start()

    for load in loads:
        load.start()

    def indices(b, carry):
        for k in range(NB):
            n = neighbours[g * MINE + b, k]
            rel = lax.rem(lax.div(n, BPS) - s + 1 + SLABS, SLABS)
            ids[b * NB + k] = jnp.minimum(rel, 2) * BPS + lax.rem(n, BPS)
        return carry

    pl.semaphore_wait(barrier, len(peers))

    def send(src, dst, sem, device):
        return pltpu.make_async_remote_copy(
            src, dst, ssem.at[sem], rsem.at[sem], device_id=device, device_id_type=MESH
        )

    def slot(buf, d, i):
        return buf[i // HALF].at[pl.ds(d * BPS + c * (BPS // 2) + (i % HALF) * CB, CB)]

    def mine(i):
        return slot(near, 1, i)

    def exchange(i):
        return send(mine(i), slot(far, 1, i), EX + i, across)

    def near_halo(d, i):
        return send(mine(i), slot(near, 2 * d, i), NEAR + d * CHUNKS + i, (sides[d], g))

    def chunk(e, i):
        return passing.at[e, pl.ds(i * CB, CB)]

    def hand(e, i):
        return send(mine(i), chunk(e, i), XS + e * CHUNKS + i, xpeer[e])

    def forward(e, i):
        base = (NEAR, FAR)[e] + de * CHUNKS + i
        return send(chunk(e, i), slot((near, far)[e], 2 * de, i), base, beyond)

    def forward_across(i):
        return send(chunk(i % 2, i), slot(far, 1, i), EX + i, xpeer[1 - i % 2])

    def far_relay(d, i):
        return send(slot(far, 1, i), slot(far, 2 * d, i), FAR + d * CHUNKS + i, (sides[d], g))

    def to_partner(buf, d, i, sem):
        return send(slot(buf, d, i), slot(buf, d, i), sem, partner)

    def own_copy(p, k=0):
        first = BPS + (BPS // 2) * (1 - c if p == 0 else c)
        piece = near[k].at[pl.ds(first, BPS // 2)]
        return send(piece, piece, OWN + p, partner)

    place_own(0).wait()
    for k in range(2):
        @pl.when(c == k)
        def _():
            for p in range(2):
                own_copy(p, k).start()

    @pl.when(c == 1)
    def _():
        own_copy(0).wait_recv()

    def begin(chunks):
        @pl.when(jnp.logical_not(on_edge))
        def _():
            for i in chunks:
                exchange(i).start()

    @pl.when(on_edge)
    def _():
        for i in range(AHEAD):
            for e in range(2):
                hand(e, i).start()

    begin(range(HALF))
    for d in range(2):
        @pl.when(inner[d])
        def _():
            for i in range(EARLY):
                near_halo(d, i).start()

    @pl.when(c == 0)
    def _():
        own_copy(0).wait_recv()

    begin(range(HALF, CHUNKS))
    loads[3 + MINE].wait()
    lax.fori_loop(0, MINE, indices, 0)

    def prepare(b):
        loads[3 + b].wait()
        relayout(x, stage, b)
        assemble(stage, a, b)


    def far_forward(col):
        for i in range(col * HALF, (col + 1) * HALF):
            for d in range(2):
                far_relay(d, i).wait_recv()
                to_partner(far, 2 * d, i, FARC + d * CHUNKS + i).start()

    def far_image(col, b):
        r = jnp.where(col == c, 0, 1)
        return send(out_far.at[col, b], image.at[g * MINE + b], IMGF + r * MINE + b, here(1 - h, col))

    def far_multiply(col):
        for i in range(col * HALF, (col + 1) * HALF):
            to_partner(far, 1, i, EXC + i).wait_recv()
            for d in range(2):
                to_partner(far, 2 * d, i, FARC + d * CHUNKS + i).wait_recv()
        multiply(ids, a, far[col], out_far.at[col], lambda b: far_image(col, b).start())

    def near_image(b):
        return send(out_near.at[1 - c, b], image.at[g * MINE + b], IMG + b, partner)

    def near_forward(col):
        for i in range(col * HALF, (col + 1) * HALF):
            for d in range(2):
                near_halo(d, i).wait_recv()
                to_partner(near, 2 * d, i, NEARC + d * CHUNKS + i).start()

    def near_multiply(col):
        if col == 0:
            own_copy(1).wait_recv()
        for i in range(col * HALF, (col + 1) * HALF):
            for d in range(2):
                to_partner(near, 2 * d, i, NEARC + d * CHUNKS + i).wait_recv()

        def after(b):
            @pl.when(c != col)
            def _():
                near_image(b).start()

        multiply(ids, a, near[col], out_near.at[col], after)

    for i in range(CHUNKS + LAG):
        if i < CHUNKS:
            @pl.when(on_edge)
            def _():
                for e in range(2):
                    hand(e, i).wait_recv()
                forward_across(i).start()
                for e in range(2):
                    if i + AHEAD < CHUNKS:
                        hand(e, i + AHEAD).start()
                    forward(e, i).start()

        if i >= LAG:
            j = i - LAG
            exchange(j).wait_recv()
            for d in range(2):
                @pl.when(inner[d])
                def _():
                    far_relay(d, j).start()
                    @pl.when(on_edge)
                    def _():
                        if j + EARLY < CHUNKS:
                            near_halo(d, j + EARLY).start()

                    if j == CHUNKS - 1:
                        @pl.when(jnp.logical_not(on_edge))
                        def _():
                            for k in range(EARLY, CHUNKS):
                                near_halo(d, k).start()
            to_partner(far, 1, j, EXC + j).start()
            if j < MINE:
                prepare(j)
            if j == HALF:
                near_forward(0)
            if j == CHUNKS - 2:
                far_forward(0)

    near_multiply(0)
    far_multiply(0)
    far_forward(1)
    far_multiply(1)
    near_forward(1)
    near_multiply(1)

    for k in range(3):
        loads[k].wait()

    def finish(first, source, at):
        def body(b, sums):
            blk = first + b
            value = 2.0 * source[at + b] - prev[blk]
            t_next[blk] = value
            fold = lambda v: jnp.sum(v.reshape(BS // 8, 8, COLS), axis=0)
            return (
                sums[0] + fold(probe[blk] * value),
                sums[1] + fold(own[blk].astype(jnp.float32) * value),
            )

        return body

    def finish_all(first, source, at, sums):
        return lax.fori_loop(0, MINE, finish(first, source, at), sums)

    zero = jnp.zeros((8, COLS), jnp.float32)
    sums = finish_all(g * MINE, out_near.at[c], 0, (zero, zero))
    first = (h * 2 + 1 - c) * MINE
    for b in range(MINE):
        near_image(b).wait_recv()
    sums = finish_all(first, image, first, sums)

    def arrived(b, sums):
        for r in range(2):
            send(out_far.at[0, b], image.at[b], IMGF + r * MINE + b, across).wait_recv()
            first = ((1 - h) * 2 + (c if r == 0 else 1 - c)) * MINE
            sums = finish(first, image, first)(b, sums)
        return sums

    sums = lax.fori_loop(0, MINE, arrived, sums)

    top = lax.broadcasted_iota(jnp.int32, (8, COLS), 0)
    pack = lambda p, q: jnp.where(
        top == 0, jnp.sum(p, axis=0, keepdims=True), jnp.where(top == 1, jnp.sum(q, axis=0, keepdims=True), 0.0)
    )

    def spread(buf, me, peer, sem, value):
        buf[me] = value
        copies = [send(buf.at[me], buf.at[me], sem + o, peer(o)) for o in range(1, 8)]
        for copy in copies:
            copy.start()
        for copy in copies:
            copy.wait_recv()
        total = buf[0]
        for i in range(1, 8):
            total = total + buf[i]
        return total, copies

    part, copies1 = spread(sums1, z, zpeer, M1, pack(*sums))
    whole, copies2 = spread(sums2, row, rpeer, M2, part)
    factor = 1.0 / math.sqrt(SLABS * BPS * BS)
    moments[...] = whole[0:2] * factor

    for p in range(2):
        own_copy(p).wait_send()
    for b in range(MINE):
        near_image(b).wait_send()
        for col in range(2):
            far_image(col, b).wait_send()
    for i in range(CHUNKS):
        @pl.when(on_edge)
        def _():
            for e in range(2):
                hand(e, i).wait_send()
                forward(e, i).wait_send()
            forward_across(i).wait_send()

        @pl.when(jnp.logical_not(on_edge))
        def _():
            exchange(i).wait_send()

        to_partner(far, 1, i, EXC + i).wait_send()
        for d in range(2):
            @pl.when(inner[d])
            def _():
                near_halo(d, i).wait_send()
                far_relay(d, i).wait_send()

            to_partner(far, 2 * d, i, FARC + d * CHUNKS + i).wait_send()
            to_partner(near, 2 * d, i, NEARC + d * CHUNKS + i).wait_send()
    for copy in copies1 + copies2:
        copy.wait_send()


def shards(tiles, neighbours, t_cur, t_prev, probes):
    f32, bf16 = jnp.float32, jnp.bfloat16
    anywhere = pl.BlockSpec(memory_space=pl.ANY)
    vmem = pl.BlockSpec(memory_space=pltpu.VMEM)
    return pl.pallas_call(
        kernel,
        out_shape=(
            jax.ShapeDtypeStruct((BPS, BS, COLS), f32),
            jax.ShapeDtypeStruct((2, COLS), f32),
        ),
        in_specs=[anywhere] * 5,
        out_specs=(vmem, vmem),
        scratch_shapes=[
            pltpu.VMEM((MINE, NB, BS * BS), bf16),
            pltpu.VMEM((NB * PITCH, LANES), f32),
            pltpu.VMEM((MINE, BS, KPAD), bf16),
            *[pltpu.VMEM((3 * BPS, BS, COLS), bf16)] * 4,
            pltpu.VMEM((BPS, BS, COLS), bf16),
            pltpu.VMEM((2, MINE, BS, COLS), f32),
            pltpu.VMEM((2, MINE, BS, COLS), f32),
            pltpu.VMEM((BPS, BS, COLS), f32),
            pltpu.VMEM((2, BPS, BS, COLS), bf16),
            pltpu.VMEM((BPS, BS, COLS), f32),
            pltpu.VMEM((BPS, BS, COLS), f32),
            pltpu.SMEM((BPS, NB), jnp.int32),
            pltpu.SMEM((MINE * NB,), jnp.int32),
            pltpu.VMEM((8, 8, COLS), f32),
            pltpu.VMEM((8, 8, COLS), f32),
            pltpu.SemaphoreType.DMA((5 + MINE,)),
            pltpu.SemaphoreType.DMA((NSEM,)),
            pltpu.SemaphoreType.DMA((NSEM,)),
        ],
        compiler_params=pltpu.CompilerParams(
            collective_id=0, has_side_effects=True, vmem_limit_bytes=60 << 20
        ),
        name="chebyshev_step",
    )(neighbours, tiles, t_cur, t_prev, probes)


def solution(mesh):
    placed = (
        P(("slab", "grp"), None, None),
        P("slab", None),
        P("slab", None, "grp"),
        P("slab", None, "grp"),
        P("slab", None, "grp"),
    )
    return jax.shard_map(
        shards,
        mesh=mesh,
        in_specs=placed,
        out_specs=(P("slab", None, "grp"), P(None, "grp")),
        check_vma=False,
    )
```

```python
import functools
import math

import jax
import jax.numpy as jnp
from jax import lax
from jax.experimental import pallas as pl
from jax.experimental.pallas import tpu as pltpu
from jax.sharding import PartitionSpec as P

MESH = pl.DeviceIdType.MESH
BPS, BS, NB = 12, 192, 27
MINE = 3
COLS = 128
LANES = 128
FLAT = BS * BS // LANES
PITCH = FLAT + 1
KPAD = 5248
CHUNKS = 6
LAG = 2
AHEAD = 3
EARLY = 3
HALF = CHUNKS // 2
CB = BPS // CHUNKS
SLABS, ZS = 64, 8


class Sems:
    def __init__(self):
        self.n = 0

    def take(self, *dims):
        size = math.prod(dims) if dims else 1
        start = self.n
        self.n += size
        return start


RX = Sems()
EX, OWN, EXC = RX.take(CHUNKS), RX.take(2), RX.take(CHUNKS)
NEAR, FAR, NEARC, FARC, XS = [RX.take(2, CHUNKS) for _ in range(5)]
IMG, IMGF, M1, M2 = RX.take(MINE), RX.take(2, MINE), RX.take(8), RX.take(8)
NSEM = RX.n


def relayout(x, stage, b):
    step = 12

    def spread(m, carry):
        for u in range(step):
            j = m * step + u
            v = x[b, :, pl.ds(pl.multiple_of(j * LANES, LANES), LANES)]
            stage[pl.ds(j, NB, stride=PITCH), :] = v.astype(jnp.float32)
        return carry

    lax.fori_loop(0, FLAT // step, spread, 0)


def assemble(stage, a, b):
    low = lax.broadcasted_iota(jnp.int32, (BS // 2, LANES), 1) < 64
    load = lambda k, i: stage[pl.ds(k * PITCH + i, BS // 2, stride=3), :]
    turn = lambda v: pltpu.roll(v, 64, 1)

    def pair(p, last):
        k = 2 * p
        e0, e1, e2 = [load(k, i) for i in range(3)]
        if last:
            zero = jnp.zeros_like(e0)
            f1, f2, rf0, rf1 = zero, zero, zero, zero
        else:
            f0, f1, f2 = [load(k + 1, i) for i in range(3)]
            rf0, rf1 = turn(f0), turn(f1)
        re1, re2 = turn(e1), turn(e2)
        even = [e0, jnp.where(low, e1, rf0), jnp.where(low, rf0, rf1)]
        odd = [jnp.where(low, re1, re2), jnp.where(low, re2, f1), f2]
        for t in range(2 if last else 3):
            at = pl.ds(pl.multiple_of(p * 384 + 128 * t, 128), LANES)
            a[b, 0 : BS // 2, at] = even[t].astype(jnp.bfloat16)
            a[b, BS // 2 : BS, at] = odd[t].astype(jnp.bfloat16)

    def body(p, carry):
        pair(p, False)
        return carry

    lax.fori_loop(0, NB // 2, body, 0)
    pair(NB // 2, True)


def multiply(ids, a, col, out, after):
    def one(b, carry):
        total = None
        for first in range(0, NB, 4):
            parts = [col[ids[b * NB + k]] for k in range(first, min(first + 4, NB))]
            if len(parts) == 3:
                parts.append(jnp.zeros((64, COLS), jnp.bfloat16))
            right = jnp.concatenate(parts, axis=0)
            left = a[b, :, first * BS : first * BS + right.shape[0]]
            term = jnp.dot(left, right, preferred_element_type=jnp.float32)
            total = term if total is None else total + term
        half = BS // 2
        for e in range(2):
            out[b, pl.ds(e, half, stride=2), :] = total[half * e : half * (e + 1)]
        after(b)
        return carry

    lax.fori_loop(0, MINE, one, 0)


def kernel(
    table, tiles, t_cur, t_prev, probes, t_next, moments,
    x, stage, a, near0, near1, far0, far1, own, result, out_far, out_near, image, passing, prev, probe, neighbours, ids, sums1, sums2,
    local, ssem, rsem,
):
    near, far = (near0, near1), (far0, far1)
    s, g = lax.axis_index("slab"), lax.axis_index("grp")
    z = lax.rem(s, ZS)
    row = lax.div(s, ZS)
    h, c = lax.div(g, 2), lax.rem(g, 2)
    up, down = lax.rem(s + 1, SLABS), lax.rem(s + SLABS - 1, SLABS)
    here = lambda hh, cc: (s, hh * 2 + cc)
    partner, across, cross = here(h, 1 - c), here(1 - h, c), here(1 - h, 1 - c)
    zpeer = lambda o: (row * ZS + lax.rem(z + o, ZS), g)
    rpeer = lambda o: (lax.rem(row + o, 8) * ZS + z, g)
    other = (1 - h) * 2 + c
    beside = lambda slab: slab + ZS - 2 * ZS * lax.rem(lax.div(slab, ZS), 2)
    sx = beside(s)
    xpeer = ((sx, g), (sx, other))
    sides = (up, down)
    edge = (z == ZS - 1, z == 0)
    on_edge = jnp.logical_or(edge[0], edge[1])
    inner = [jnp.logical_not(e) for e in edge]
    de = jnp.where(edge[1], 1, 0)
    beyond = (lax.rem(jnp.where(edge[1], sx + SLABS - 1, sx + 1), SLABS), g)
    greet = [(jnp.where(edge[d], beside(sides[d]), sides[d]), g) for d in range(2)]

    loads = [
        pltpu.make_async_copy(t_cur, own, local.at[0]),
        pltpu.make_async_copy(t_prev, prev, local.at[1]),
        pltpu.make_async_copy(probes, probe, local.at[2]),
    ] + [pltpu.make_async_copy(tiles.at[b], x.at[b], local.at[3 + b]) for b in range(MINE)]
    loads.append(pltpu.make_async_copy(table, neighbours, local.at[3 + MINE]))

    barrier = pltpu.get_barrier_semaphore()
    peers = [partner, across, cross]
    peers += greet + list(xpeer)
    peers += [zpeer(o) for o in range(1, ZS)] + [rpeer(o) for o in range(1, 8)]
    for peer in peers:
        pl.semaphore_signal(barrier, 1, device_id=peer, device_id_type=MESH)
    def place_own(k):
        return pltpu.make_async_copy(t_cur, near[k].at[pl.ds(BPS, BPS)], local.at[4 + MINE])

    for k in range(2):
        @pl.when(c == k)
        def _():
            place_own(k).start()

    for load in loads:
        load.start()

    def indices(b, carry):
        for k in range(NB):
            n = neighbours[g * MINE + b, k]
            rel = lax.rem(lax.div(n, BPS) - s + 1 + SLABS, SLABS)
            ids[b * NB + k] = jnp.minimum(rel, 2) * BPS + lax.rem(n, BPS)
        return carry

    pl.semaphore_wait(barrier, len(peers))

    def send(src, dst, sem, device):
        return pltpu.make_async_remote_copy(
            src, dst, ssem.at[sem], rsem.at[sem], device_id=device, device_id_type=MESH
        )

    def slot(buf, d, i):
        return buf[i // HALF].at[pl.ds(d * BPS + c * (BPS // 2) + (i % HALF) * CB, CB)]

    def mine(i):
        return slot(near, 1, i)

    def exchange(i):
        return send(mine(i), slot(far, 1, i), EX + i, across)

    def near_halo(d, i):
        return send(mine(i), slot(near, 2 * d, i), NEAR + d * CHUNKS + i, (sides[d], g))

    def chunk(e, i):
        return passing.at[e, pl.ds(i * CB, CB)]

    def hand(e, i):
        return send(mine(i), chunk(e, i), XS + e * CHUNKS + i, xpeer[e])

    def forward(e, i):
        base = (NEAR, FAR)[e] + de * CHUNKS + i
        return send(chunk(e, i), slot((near, far)[e], 2 * de, i), base, beyond)

    def forward_across(i):
        return send(chunk(i % 2, i), slot(far, 1, i), EX + i, xpeer[1 - i % 2])

    def far_relay(d, i):
        return send(slot(far, 1, i), slot(far, 2 * d, i), FAR + d * CHUNKS + i, (sides[d], g))

    def to_partner(buf, d, i, sem):
        return send(slot(buf, d, i), slot(buf, d, i), sem, partner)

    def own_copy(p, k=0):
        first = BPS + (BPS // 2) * (1 - c if p == 0 else c)
        piece = near[k].at[pl.ds(first, BPS // 2)]
        return send(piece, piece, OWN + p, partner)

    place_own(0).wait()
    for k in range(2):
        @pl.when(c == k)
        def _():
            for p in range(2):
                own_copy(p, k).start()

    @pl.when(c == 1)
    def _():
        own_copy(0).wait_recv()

    def begin(chunks):
        @pl.when(jnp.logical_not(on_edge))
        def _():
            for i in chunks:
                exchange(i).start()

    @pl.when(on_edge)
    def _():
        for i in range(AHEAD):
            for e in range(2):
                hand(e, i).start()

    begin(range(HALF))
    for d in range(2):
        @pl.when(inner[d])
        def _():
            for i in range(EARLY):
                near_halo(d, i).start()

    @pl.when(c == 0)
    def _():
        own_copy(0).wait_recv()

    begin(range(HALF, CHUNKS))
    loads[3 + MINE].wait()
    lax.fori_loop(0, MINE, indices, 0)

    def prepare(b):
        loads[3 + b].wait()
        relayout(x, stage, b)
        assemble(stage, a, b)


    def far_forward(col):
        for i in range(col * HALF, (col + 1) * HALF):
            for d in range(2):
                far_relay(d, i).wait_recv()
                to_partner(far, 2 * d, i, FARC + d * CHUNKS + i).start()

    def far_image(col, b):
        r = jnp.where(col == c, 0, 1)
        return send(out_far.at[col, b], image.at[g * MINE + b], IMGF + r * MINE + b, here(1 - h, col))

    def far_multiply(col):
        for i in range(col * HALF, (col + 1) * HALF):
            to_partner(far, 1, i, EXC + i).wait_recv()
            for d in range(2):
                to_partner(far, 2 * d, i, FARC + d * CHUNKS + i).wait_recv()
        multiply(ids, a, far[col], out_far.at[col], lambda b: far_image(col, b).start())

    def near_image(b):
        return send(out_near.at[1 - c, b], image.at[g * MINE + b], IMG + b, partner)

    def near_forward(col):
        for i in range(col * HALF, (col + 1) * HALF):
            for d in range(2):
                near_halo(d, i).wait_recv()
                to_partner(near, 2 * d, i, NEARC + d * CHUNKS + i).start()

    def near_multiply(col):
        if col == 0:
            own_copy(1).wait_recv()
        for i in range(col * HALF, (col + 1) * HALF):
            for d in range(2):
                to_partner(near, 2 * d, i, NEARC + d * CHUNKS + i).wait_recv()

        def after(b):
            @pl.when(c != col)
            def _():
                near_image(b).start()

        multiply(ids, a, near[col], out_near.at[col], after)

    prepare(0)

    for i in range(CHUNKS + LAG):
        if i < CHUNKS:
            @pl.when(on_edge)
            def _():
                for e in range(2):
                    hand(e, i).wait_recv()
                forward_across(i).start()
                for e in range(2):
                    if i + AHEAD < CHUNKS:
                        hand(e, i + AHEAD).start()
                    forward(e, i).start()

        if i >= LAG:
            j = i - LAG
            exchange(j).wait_recv()
            for d in range(2):
                @pl.when(inner[d])
                def _():
                    far_relay(d, j).start()
                    @pl.when(on_edge)
                    def _():
                        if j + EARLY < CHUNKS:
                            near_halo(d, j + EARLY).start()

                    if j == CHUNKS - 1:
                        @pl.when(jnp.logical_not(on_edge))
                        def _():
                            for k in range(EARLY, CHUNKS):
                                near_halo(d, k).start()
            to_partner(far, 1, j, EXC + j).start()
            if j < MINE - 1:
                prepare(j + 1)
            if j == CHUNKS - 1:
                near_forward(0)
                far_forward(0)

    near_multiply(0)
    far_multiply(0)
    far_forward(1)
    far_multiply(1)
    near_forward(1)
    near_multiply(1)

    for k in range(3):
        loads[k].wait()

    def finish(first, source, at):
        def body(b, sums):
            blk = first + b
            value = 2.0 * source[at + b] - prev[blk]
            result[blk] = value
            fold = lambda v: jnp.sum(v.reshape(BS // 8, 8, COLS), axis=0)
            return (
                sums[0] + fold(probe[blk] * value),
                sums[1] + fold(own[blk].astype(jnp.float32) * value),
            )

        return body

    def finish_all(first, source, at, sums):
        return lax.fori_loop(0, MINE, finish(first, source, at), sums)

    zero = jnp.zeros((8, COLS), jnp.float32)
    sums = finish_all(g * MINE, out_near.at[c], 0, (zero, zero))
    first = (h * 2 + 1 - c) * MINE
    for b in range(MINE):
        near_image(b).wait_recv()
    sums = finish_all(first, image, first, sums)

    def store(k):
        rows = pl.ds((h if k == 0 else 1 - h) * 2 * MINE, 2 * MINE)
        return pltpu.make_async_copy(result.at[rows], t_next.at[rows], local.at[5 + MINE + k])

    store(0).start()

    def arrived(b, sums):
        for r in range(2):
            send(out_far.at[0, b], image.at[b], IMGF + r * MINE + b, across).wait_recv()
            first = ((1 - h) * 2 + (c if r == 0 else 1 - c)) * MINE
            sums = finish(first, image, first)(b, sums)
        return sums

    sums = lax.fori_loop(0, MINE, arrived, sums)
    store(1).start()

    top = lax.broadcasted_iota(jnp.int32, (8, COLS), 0)
    pack = lambda p, q: jnp.where(
        top == 0, jnp.sum(p, axis=0, keepdims=True), jnp.where(top == 1, jnp.sum(q, axis=0, keepdims=True), 0.0)
    )

    def spread(buf, me, peer, sem, value):
        buf[me] = value
        copies = [send(buf.at[me], buf.at[me], sem + o, peer(o)) for o in range(1, 8)]
        for copy in copies:
            copy.start()
        for copy in copies:
            copy.wait_recv()
        total = buf[0]
        for i in range(1, 8):
            total = total + buf[i]
        return total, copies

    part, copies1 = spread(sums1, z, zpeer, M1, pack(*sums))
    whole, copies2 = spread(sums2, row, rpeer, M2, part)
    factor = 1.0 / math.sqrt(SLABS * BPS * BS)
    moments[...] = whole[0:2] * factor

    for p in range(2):
        store(p).wait()
        own_copy(p).wait_send()
    for b in range(MINE):
        near_image(b).wait_send()
        for col in range(2):
            far_image(col, b).wait_send()
    for i in range(CHUNKS):
        @pl.when(on_edge)
        def _():
            for e in range(2):
                hand(e, i).wait_send()
                forward(e, i).wait_send()
            forward_across(i).wait_send()

        @pl.when(jnp.logical_not(on_edge))
        def _():
            exchange(i).wait_send()

        to_partner(far, 1, i, EXC + i).wait_send()
        for d in range(2):
            @pl.when(inner[d])
            def _():
                near_halo(d, i).wait_send()
                far_relay(d, i).wait_send()

            to_partner(far, 2 * d, i, FARC + d * CHUNKS + i).wait_send()
            to_partner(near, 2 * d, i, NEARC + d * CHUNKS + i).wait_send()
    for copy in copies1 + copies2:
        copy.wait_send()


def hand_over(value, sums, t_next, moments):
    t_next[...] = value[...]
    moments[...] = sums[...]


def shards(tiles, neighbours, t_cur, t_prev, probes):
    f32, bf16 = jnp.float32, jnp.bfloat16
    anywhere = pl.BlockSpec(memory_space=pl.ANY)
    vmem = pl.BlockSpec(memory_space=pltpu.VMEM)
    t_next, moments = pl.pallas_call(
        kernel,
        out_shape=(
            jax.ShapeDtypeStruct((BPS, BS, COLS), f32),
            jax.ShapeDtypeStruct((2, COLS), f32),
        ),
        in_specs=[anywhere] * 5,
        out_specs=(anywhere, vmem),
        scratch_shapes=[
            pltpu.VMEM((MINE, NB, BS * BS), bf16),
            pltpu.VMEM((NB * PITCH, LANES), f32),
            pltpu.VMEM((MINE, BS, KPAD), bf16),
            *[pltpu.VMEM((3 * BPS, BS, COLS), bf16)] * 4,
            pltpu.VMEM((BPS, BS, COLS), bf16),
            pltpu.VMEM((BPS, BS, COLS), f32),
            pltpu.VMEM((2, MINE, BS, COLS), f32),
            pltpu.VMEM((2, MINE, BS, COLS), f32),
            pltpu.VMEM((BPS, BS, COLS), f32),
            pltpu.VMEM((2, BPS, BS, COLS), bf16),
            pltpu.VMEM((BPS, BS, COLS), f32),
            pltpu.VMEM((BPS, BS, COLS), f32),
            pltpu.SMEM((BPS, NB), jnp.int32),
            pltpu.SMEM((MINE * NB,), jnp.int32),
            pltpu.VMEM((8, 8, COLS), f32),
            pltpu.VMEM((8, 8, COLS), f32),
            pltpu.SemaphoreType.DMA((7 + MINE,)),
            pltpu.SemaphoreType.DMA((NSEM,)),
            pltpu.SemaphoreType.DMA((NSEM,)),
        ],
        compiler_params=pltpu.CompilerParams(
            collective_id=0, has_side_effects=True, vmem_limit_bytes=60 << 20
        ),
        name="chebyshev_step",
    )(neighbours, tiles, t_cur, t_prev, probes)
    block = pl.BlockSpec((MINE, BS, COLS), lambda i: (i, 0, 0))
    small = pl.BlockSpec((2, COLS), lambda i: (0, 0))
    return pl.pallas_call(
        hand_over,
        grid=(BPS // MINE,),
        out_shape=(
            jax.ShapeDtypeStruct((BPS, BS, COLS), f32),
            jax.ShapeDtypeStruct((2, COLS), f32),
        ),
        in_specs=[block, small],
        out_specs=(block, small),
        name="hand_over",
    )(t_next, moments)


def solution(mesh):
    placed = (
        P(("slab", "grp"), None, None),
        P("slab", None),
        P("slab", None, "grp"),
        P("slab", None, "grp"),
        P("slab", None, "grp"),
    )
    return jax.shard_map(
        shards,
        mesh=mesh,
        in_specs=placed,
        out_specs=(P("slab", None, "grp"), P(None, "grp")),
        check_vma=False,
    )
```

```python
import functools
import math

import jax
import jax.numpy as jnp
from jax import lax
from jax.experimental import pallas as pl
from jax.experimental.pallas import tpu as pltpu
from jax.sharding import PartitionSpec as P

MESH = pl.DeviceIdType.MESH
BPS, BS, NB = 12, 192, 27
MINE = 3
COLS = 128
LANES = 128
FLAT = BS * BS // LANES
PITCH = FLAT + 1
KPAD = 5248
CHUNKS = 6
LAG = 2
AHEAD = 3
EARLY = 3
HALF = CHUNKS // 2
CB = BPS // CHUNKS
SLABS, ZS = 64, 8


class Sems:
    def __init__(self):
        self.n = 0

    def take(self, *dims):
        size = math.prod(dims) if dims else 1
        start = self.n
        self.n += size
        return start


RX = Sems()
EX, OWN, EXC = RX.take(CHUNKS), RX.take(2), RX.take(CHUNKS)
NEAR, FAR, NEARC, FARC, XS = [RX.take(2, CHUNKS) for _ in range(5)]
IMG, IMGF, M1, M2 = RX.take(MINE), RX.take(2, MINE), RX.take(8), RX.take(8)
NSEM = RX.n


def relayout(x, stage, b):
    step = 12

    def spread(m, carry):
        for u in range(step):
            j = m * step + u
            v = x[b, :, pl.ds(pl.multiple_of(j * LANES, LANES), LANES)]
            stage[pl.ds(j, NB, stride=PITCH), :] = v.astype(jnp.float32)
        return carry

    lax.fori_loop(0, FLAT // step, spread, 0)


def assemble(stage, a, b):
    low = lax.broadcasted_iota(jnp.int32, (BS // 2, LANES), 1) < 64
    load = lambda k, i: stage[pl.ds(k * PITCH + i, BS // 2, stride=3), :]
    turn = lambda v: pltpu.roll(v, 64, 1)

    def pair(p, last):
        k = 2 * p
        e0, e1, e2 = [load(k, i) for i in range(3)]
        if last:
            zero = jnp.zeros_like(e0)
            f1, f2, rf0, rf1 = zero, zero, zero, zero
        else:
            f0, f1, f2 = [load(k + 1, i) for i in range(3)]
            rf0, rf1 = turn(f0), turn(f1)
        re1, re2 = turn(e1), turn(e2)
        even = [e0, jnp.where(low, e1, rf0), jnp.where(low, rf0, rf1)]
        odd = [jnp.where(low, re1, re2), jnp.where(low, re2, f1), f2]
        for t in range(2 if last else 3):
            at = pl.ds(pl.multiple_of(p * 384 + 128 * t, 128), LANES)
            a[b, 0 : BS // 2, at] = even[t].astype(jnp.bfloat16)
            a[b, BS // 2 : BS, at] = odd[t].astype(jnp.bfloat16)

    def body(p, carry):
        pair(p, False)
        return carry

    lax.fori_loop(0, NB // 2, body, 0)
    pair(NB // 2, True)


def multiply(ids, a, col, out, after):
    def one(b, carry):
        total = None
        for first in range(0, NB, 4):
            parts = [col[ids[b * NB + k]] for k in range(first, min(first + 4, NB))]
            if len(parts) == 3:
                parts.append(jnp.zeros((64, COLS), jnp.bfloat16))
            right = jnp.concatenate(parts, axis=0)
            left = a[b, :, first * BS : first * BS + right.shape[0]]
            term = jnp.dot(left, right, preferred_element_type=jnp.float32)
            total = term if total is None else total + term
        half = BS // 2
        for e in range(2):
            out[b, pl.ds(e, half, stride=2), :] = total[half * e : half * (e + 1)]
        after(b)
        return carry

    lax.fori_loop(0, MINE, one, 0)


def kernel(
    table, tiles, t_cur, t_prev, probes, t_next, moments,
    x, stage, a, near0, near1, far0, far1, own, result, out_far, out_near, image, passing, prev, probe, neighbours, ids, sums1, sums2,
    local, ssem, rsem,
):
    near, far = (near0, near1), (far0, far1)
    s, g = lax.axis_index("slab"), lax.axis_index("grp")
    z = lax.rem(s, ZS)
    row = lax.div(s, ZS)
    h, c = lax.div(g, 2), lax.rem(g, 2)
    up, down = lax.rem(s + 1, SLABS), lax.rem(s + SLABS - 1, SLABS)
    here = lambda hh, cc: (s, hh * 2 + cc)
    partner, across, cross = here(h, 1 - c), here(1 - h, c), here(1 - h, 1 - c)
    zpeer = lambda o: (row * ZS + lax.rem(z + o, ZS), g)
    rpeer = lambda o: (lax.rem(row + o, 8) * ZS + z, g)
    other = (1 - h) * 2 + c
    beside = lambda slab: slab + ZS - 2 * ZS * lax.rem(lax.div(slab, ZS), 2)
    sx = beside(s)
    xpeer = ((sx, g), (sx, other))
    sides = (up, down)
    edge = (z == ZS - 1, z == 0)
    on_edge = jnp.logical_or(edge[0], edge[1])
    inner = [jnp.logical_not(e) for e in edge]
    de = jnp.where(edge[1], 1, 0)
    beyond = (lax.rem(jnp.where(edge[1], sx + SLABS - 1, sx + 1), SLABS), g)
    greet = [(jnp.where(edge[d], beside(sides[d]), sides[d]), g) for d in range(2)]

    loads = [
        pltpu.make_async_copy(t_cur, own, local.at[0]),
        pltpu.make_async_copy(t_prev, prev, local.at[1]),
        pltpu.make_async_copy(probes, probe, local.at[2]),
    ] + [pltpu.make_async_copy(tiles.at[b], x.at[b], local.at[3 + b]) for b in range(MINE)]
    loads.append(pltpu.make_async_copy(table, neighbours, local.at[3 + MINE]))

    barrier = pltpu.get_barrier_semaphore()
    peers = [partner, across, cross]
    peers += greet + list(xpeer)
    peers += [zpeer(o) for o in range(1, ZS)] + [rpeer(o) for o in range(1, 8)]
    for peer in peers:
        pl.semaphore_signal(barrier, 1, device_id=peer, device_id_type=MESH)
    def place_own(k):
        return pltpu.make_async_copy(t_cur, near[k].at[pl.ds(BPS, BPS)], local.at[4 + MINE])

    for k in range(2):
        @pl.when(c == k)
        def _():
            place_own(k).start()

    for load in loads:
        load.start()

    def indices(b, carry):
        for k in range(NB):
            n = neighbours[g * MINE + b, k]
            rel = lax.rem(lax.div(n, BPS) - s + 1 + SLABS, SLABS)
            ids[b * NB + k] = jnp.minimum(rel, 2) * BPS + lax.rem(n, BPS)
        return carry

    pl.semaphore_wait(barrier, len(peers))

    def send(src, dst, sem, device):
        return pltpu.make_async_remote_copy(
            src, dst, ssem.at[sem], rsem.at[sem], device_id=device, device_id_type=MESH
        )

    def slot(buf, d, i):
        return buf[i // HALF].at[pl.ds(d * BPS + c * (BPS // 2) + (i % HALF) * CB, CB)]

    def mine(i):
        return slot(near, 1, i)

    def exchange(i):
        return send(mine(i), slot(far, 1, i), EX + i, across)

    def near_halo(d, i):
        return send(mine(i), slot(near, 2 * d, i), NEAR + d * CHUNKS + i, (sides[d], g))

    def chunk(e, i):
        return passing.at[e, pl.ds(i * CB, CB)]

    def hand(e, i):
        return send(mine(i), chunk(e, i), XS + e * CHUNKS + i, xpeer[e])

    def forward(e, i):
        base = (NEAR, FAR)[e] + de * CHUNKS + i
        return send(chunk(e, i), slot((near, far)[e], 2 * de, i), base, beyond)

    def forward_across(i):
        return send(chunk(i % 2, i), slot(far, 1, i), EX + i, xpeer[1 - i % 2])

    def far_relay(d, i):
        return send(slot(far, 1, i), slot(far, 2 * d, i), FAR + d * CHUNKS + i, (sides[d], g))

    def to_partner(buf, d, i, sem):
        return send(slot(buf, d, i), slot(buf, d, i), sem, partner)

    def own_copy(p, k=0):
        first = BPS + (BPS // 2) * (1 - c if p == 0 else c)
        piece = near[k].at[pl.ds(first, BPS // 2)]
        return send(piece, piece, OWN + p, partner)

    place_own(0).wait()
    for k in range(2):
        @pl.when(c == k)
        def _():
            for p in range(2):
                own_copy(p, k).start()

    @pl.when(c == 1)
    def _():
        own_copy(0).wait_recv()

    def begin(chunks):
        @pl.when(jnp.logical_not(on_edge))
        def _():
            for i in chunks:
                exchange(i).start()

    @pl.when(on_edge)
    def _():
        for i in range(AHEAD):
            for e in range(2):
                hand(e, i).start()

    begin(range(HALF))
    for d in range(2):
        @pl.when(inner[d])
        def _():
            for i in range(EARLY):
                near_halo(d, i).start()

    @pl.when(c == 0)
    def _():
        own_copy(0).wait_recv()

    begin(range(HALF, CHUNKS))
    loads[3 + MINE].wait()
    lax.fori_loop(0, MINE, indices, 0)

    def prepare(b):
        loads[3 + b].wait()
        relayout(x, stage, b)
        assemble(stage, a, b)


    def far_forward(col):
        for i in range(col * HALF, (col + 1) * HALF):
            for d in range(2):
                far_relay(d, i).wait_recv()
                to_partner(far, 2 * d, i, FARC + d * CHUNKS + i).start()

    def far_image(col, b):
        r = jnp.where(col == c, 0, 1)
        return send(out_far.at[col, b], image.at[g * MINE + b], IMGF + r * MINE + b, here(1 - h, col))

    def far_multiply(col):
        for i in range(col * HALF, (col + 1) * HALF):
            to_partner(far, 1, i, EXC + i).wait_recv()
            for d in range(2):
                to_partner(far, 2 * d, i, FARC + d * CHUNKS + i).wait_recv()
        multiply(ids, a, far[col], out_far.at[col], lambda b: far_image(col, b).start())

    def near_image(b):
        return send(out_near.at[1 - c, b], image.at[g * MINE + b], IMG + b, partner)

    def near_forward(col):
        for i in range(col * HALF, (col + 1) * HALF):
            for d in range(2):
                near_halo(d, i).wait_recv()
                to_partner(near, 2 * d, i, NEARC + d * CHUNKS + i).start()

    def near_multiply(col):
        if col == 0:
            own_copy(1).wait_recv()
        for i in range(col * HALF, (col + 1) * HALF):
            for d in range(2):
                to_partner(near, 2 * d, i, NEARC + d * CHUNKS + i).wait_recv()

        def after(b):
            @pl.when(c != col)
            def _():
                near_image(b).start()

        multiply(ids, a, near[col], out_near.at[col], after)

    for i in range(CHUNKS + LAG):
        if i < CHUNKS:
            @pl.when(on_edge)
            def _():
                for e in range(2):
                    hand(e, i).wait_recv()
                forward_across(i).start()
                for e in range(2):
                    if i + AHEAD < CHUNKS:
                        hand(e, i + AHEAD).start()
                    forward(e, i).start()

        if i >= LAG:
            j = i - LAG
            exchange(j).wait_recv()
            for d in range(2):
                @pl.when(inner[d])
                def _():
                    far_relay(d, j).start()
                    @pl.when(on_edge)
                    def _():
                        if j + EARLY < CHUNKS:
                            near_halo(d, j + EARLY).start()

                    if j == CHUNKS - 1:
                        @pl.when(jnp.logical_not(on_edge))
                        def _():
                            for k in range(EARLY, CHUNKS):
                                near_halo(d, k).start()
            to_partner(far, 1, j, EXC + j).start()
            if j < MINE:
                prepare(j)
            if j == HALF:
                near_forward(0)
            if j == CHUNKS - 2:
                far_forward(0)

    near_multiply(0)
    far_multiply(0)
    far_forward(1)
    far_multiply(1)
    near_forward(1)
    near_multiply(1)

    for k in range(3):
        loads[k].wait()

    def finish(first, source, at):
        def body(b, sums):
            blk = first + b
            value = 2.0 * source[at + b] - prev[blk]
            result[blk] = value
            fold = lambda v: jnp.sum(v.reshape(BS // 8, 8, COLS), axis=0)
            return (
                sums[0] + fold(probe[blk] * value),
                sums[1] + fold(own[blk].astype(jnp.float32) * value),
            )

        return body

    def finish_all(first, source, at, sums):
        return lax.fori_loop(0, MINE, finish(first, source, at), sums)

    zero = jnp.zeros((8, COLS), jnp.float32)
    sums = finish_all(g * MINE, out_near.at[c], 0, (zero, zero))
    first = (h * 2 + 1 - c) * MINE
    for b in range(MINE):
        near_image(b).wait_recv()
    sums = finish_all(first, image, first, sums)

    def store(k):
        rows = pl.ds((h if k == 0 else 1 - h) * 2 * MINE, 2 * MINE)
        return pltpu.make_async_copy(result.at[rows], t_next.at[rows], local.at[5 + MINE + k])

    store(0).start()

    def arrived(b, sums):
        for r in range(2):
            send(out_far.at[0, b], image.at[b], IMGF + r * MINE + b, across).wait_recv()
            first = ((1 - h) * 2 + (c if r == 0 else 1 - c)) * MINE
            sums = finish(first, image, first)(b, sums)
        return sums

    sums = lax.fori_loop(0, MINE, arrived, sums)
    store(1).start()

    top = lax.broadcasted_iota(jnp.int32, (8, COLS), 0)
    pack = lambda p, q: jnp.where(
        top == 0, jnp.sum(p, axis=0, keepdims=True), jnp.where(top == 1, jnp.sum(q, axis=0, keepdims=True), 0.0)
    )

    def spread(buf, me, peer, sem, value):
        buf[me] = value
        copies = [send(buf.at[me], buf.at[me], sem + o, peer(o)) for o in range(1, 8)]
        for copy in copies:
            copy.start()
        for copy in copies:
            copy.wait_recv()
        total = buf[0]
        for i in range(1, 8):
            total = total + buf[i]
        return total, copies

    part, copies1 = spread(sums1, z, zpeer, M1, pack(*sums))
    whole, copies2 = spread(sums2, row, rpeer, M2, part)
    factor = 1.0 / math.sqrt(SLABS * BPS * BS)
    moments[...] = whole[0:2] * factor

    for p in range(2):
        store(p).wait()
        own_copy(p).wait_send()
    for b in range(MINE):
        near_image(b).wait_send()
        for col in range(2):
            far_image(col, b).wait_send()
    for i in range(CHUNKS):
        @pl.when(on_edge)
        def _():
            for e in range(2):
                hand(e, i).wait_send()
                forward(e, i).wait_send()
            forward_across(i).wait_send()

        @pl.when(jnp.logical_not(on_edge))
        def _():
            exchange(i).wait_send()

        to_partner(far, 1, i, EXC + i).wait_send()
        for d in range(2):
            @pl.when(inner[d])
            def _():
                near_halo(d, i).wait_send()
                far_relay(d, i).wait_send()

            to_partner(far, 2 * d, i, FARC + d * CHUNKS + i).wait_send()
            to_partner(near, 2 * d, i, NEARC + d * CHUNKS + i).wait_send()
    for copy in copies1 + copies2:
        copy.wait_send()


def shards(tiles, neighbours, t_cur, t_prev, probes):
    f32, bf16 = jnp.float32, jnp.bfloat16
    anywhere = pl.BlockSpec(memory_space=pl.ANY)
    vmem = pl.BlockSpec(memory_space=pltpu.VMEM)
    return pl.pallas_call(
        kernel,
        out_shape=(
            jax.ShapeDtypeStruct((BPS, BS, COLS), f32),
            jax.ShapeDtypeStruct((2, COLS), f32),
        ),
        in_specs=[anywhere] * 5,
        out_specs=(anywhere, vmem),
        scratch_shapes=[
            pltpu.VMEM((MINE, NB, BS * BS), bf16),
            pltpu.VMEM((NB * PITCH, LANES), f32),
            pltpu.VMEM((MINE, BS, KPAD), bf16),
            *[pltpu.VMEM((3 * BPS, BS, COLS), bf16)] * 4,
            pltpu.VMEM((BPS, BS, COLS), bf16),
            pltpu.VMEM((BPS, BS, COLS), f32),
            pltpu.VMEM((2, MINE, BS, COLS), f32),
            pltpu.VMEM((2, MINE, BS, COLS), f32),
            pltpu.VMEM((BPS, BS, COLS), f32),
            pltpu.VMEM((2, BPS, BS, COLS), bf16),
            pltpu.VMEM((BPS, BS, COLS), f32),
            pltpu.VMEM((BPS, BS, COLS), f32),
            pltpu.SMEM((BPS, NB), jnp.int32),
            pltpu.SMEM((MINE * NB,), jnp.int32),
            pltpu.VMEM((8, 8, COLS), f32),
            pltpu.VMEM((8, 8, COLS), f32),
            pltpu.SemaphoreType.DMA((7 + MINE,)),
            pltpu.SemaphoreType.DMA((NSEM,)),
            pltpu.SemaphoreType.DMA((NSEM,)),
        ],
        compiler_params=pltpu.CompilerParams(
            collective_id=0, has_side_effects=True, vmem_limit_bytes=60 << 20
        ),
        name="chebyshev_step",
    )(neighbours, tiles, t_cur, t_prev, probes)


def solution(mesh):
    placed = (
        P(("slab", "grp"), None, None),
        P("slab", None),
        P("slab", None, "grp"),
        P("slab", None, "grp"),
        P("slab", None, "grp"),
    )
    return jax.shard_map(
        shards,
        mesh=mesh,
        in_specs=placed,
        out_specs=(P("slab", None, "grp"), P(None, "grp")),
        check_vma=False,
    )
```
